32 devices in a mesh: dom: 32 (over z, y, x, core).
Axes of the slice: x: 2, y: 2, z: 4, core: 2. Of those that a mesh axis runs over, the one named last changes fastest.
Arguments:
- coef_init: float32 [1024, 128], P('dom'), may hold values from -6 to 6
- basis: bfloat16 [49152, 1024], P('dom'), may hold values from -0.375 to 0.375
- basis_scale: float32 [384], P('dom'), may hold values from 0.5 to 2
- ext_force: float32 [49152, 128], P('dom'), may hold values from -6 to 6
- precond: float32 [1024], P('dom'), may hold values from 0.5 to 6, as said below
- connectivity: int32 [14400, 8], P('dom'), may hold values from 0 to 767, as said below
- halo_nodes: int32 [8192], P('dom'), may hold values from 0 to 511, as said below
- plastic: int32 [14400], P('dom'), may hold values 0 or 1
Outputs:
- coef_final: float32 [1024, 128], P('dom')
- nodal_residual: float32 [49152, 128], P('dom')
The draws below stay inside these ranges and needn't reach their ends.
Inputs may be any that keep to these rules, and one draw needn't show every extreme that they name: `connectivity`: each part is a structured block of 16 x 16 x 2 nodes, numbered in a part-specific order; each row lists an element's 8 corners in corner-bit order (bit 0 along x, bit 1 along y, bit 2 along z). Entries below 512 are the part's own nodes; an entry 512 + h names the node listed h-th in the next part's halo_nodes (the next part's first z layer). `halo_nodes`: the entries of one part are its own local node numbers of its first z layer, in grid order with x fastest, all distinct. `precond`: Positive.
All inputs are finite; a program needn't handle non-finite values. No bound on the sum of `plastic` on one device may be relied on, other than what follows from the above.
Results may differ from the reference program's by a relative error of at most 0.0087.
Values may be sent and summed in bfloat16 or wider, within the bound.
No kernel may reach another device: no remote copies, remote signals or barrier semaphores. Data moves between devices by JAX's collectives and lax.ppermute only.
A program may use at most 64 MiB of HBM per device.

```python
import math
import jax
import jax.numpy as jnp
from jax import lax

R = 1024
C = 128
GX = 16
GY = 16
GZ = 2
TILE = 128
ITERS = 2
NODE_DEV = 512
ELEM_DEV = 450
HALO = 256
NODES = 16384
ROWS = 49152
ELEMS = 14400
N_DOM = 32


def part_numbering(subkey):
    count = GX * GY * GZ
    scores = jax.random.randint(subkey, (count,), 0, 2 ** 18, jnp.int32) * count + jnp.arange(count, dtype=jnp.int32)
    scores = scores.at[0].set(-1).at[1].set(2 ** 30)
    order = jnp.argsort(scores, stable=True).astype(jnp.int32)
    return jnp.argsort(order, stable=True).astype(jnp.int32)


def mesh_numbering(key):
    node_keys = jax.random.split(jax.random.fold_in(key, 7), N_DOM)
    node_perm = jax.vmap(part_numbering)(node_keys)
    elem_keys = jax.random.split(jax.random.fold_in(key, 11), N_DOM)
    elem_perm = jax.vmap(lambda subkey: jax.random.permutation(subkey, (GX - 1) * (GY - 1) * GZ))(elem_keys)
    return (node_perm.astype(jnp.int32), elem_perm.astype(jnp.int32))


def draw_halo_nodes(key, part):
    node_perm, elem_perm = mesh_numbering(key)
    return node_perm[:, :GX * GY].reshape(-1).astype(jnp.int32)


def draw_connectivity(key, part):
    node_perm, elem_perm = mesh_numbering(key)
    element = jnp.arange((GX - 1) * (GY - 1) * GZ, dtype=jnp.int32)
    cell_x = element % (GX - 1)
    cell_y = element // (GX - 1) % (GY - 1)
    cell_z = element // ((GX - 1) * (GY - 1))
    corner = jnp.arange(8, dtype=jnp.int32)
    point_x = cell_x[:, None] + (corner & 1)[None, :]
    point_y = cell_y[:, None] + (corner >> 1 & 1)[None, :]
    point_z = cell_z[:, None] + (corner >> 2 & 1)[None, :]
    grid_point = jnp.minimum(point_z, GZ - 1) * GX * GY + point_y * GX + point_x
    own_index = node_perm[:, grid_point]
    halo_index = GX * GY * GZ + point_y * GX + point_x
    local_index = jnp.where(point_z[None] < GZ, own_index, halo_index[None])
    shuffled = jnp.take_along_axis(local_index, elem_perm[:, :, None], axis=1)
    return shuffled.reshape(-1, 8).astype(jnp.int32)


def draw_precond(key, part):
    position = jnp.arange(R, dtype=jnp.float32) / R
    factor = jnp.exp(jax.random.uniform(key, (R,), jnp.float32, -0.35, 0.35))
    rising = 1.0 + 2.0 * position
    return (rising * factor).astype(jnp.float32)


def plant(values, rng, low, top_value):
    extent = values.shape
    spot = [jax.random.randint(jax.random.fold_in(rng, axis), (), 0, extent[axis]) for axis in range(len(extent))]
    values = values.at[tuple(spot)].set(low)
    longest = extent.index(max(extent))
    spot[longest] = (spot[longest] + 1) % extent[longest]
    return values.at[tuple(spot)].set(top_value)


def strengthened(drawn, own_key, source, target, shards_of, factor):
    owner, partner = [(jnp.arange(drawn.shape[dim]) // (drawn.shape[dim] // shards_of)).reshape([-1 if axis == dim else 1 for axis in range(drawn.ndim)]) for dim in (source, target)]
    chosen = jax.random.permutation(own_key, shards_of)[partner]
    strong = (owner == chosen) | (owner == (partner + shards_of // 2) % shards_of)
    return jnp.where(strong, factor * drawn, drawn)


def steps_of(own_key, extent, cuts, low, largest):
    gain, own = 1.0, jax.random.fold_in(own_key, 6)
    for dim, blocks in cuts:
        heights = jnp.exp(jax.random.uniform(jax.random.fold_in(own, dim), (blocks,), jnp.float32, low / len(cuts), largest / len(cuts)))
        gain = gain * jnp.repeat(heights, extent[dim] // blocks).reshape([-1 if axis == dim else 1 for axis in range(len(extent))])
    return gain


def centred(stream_key, extent, deviation, bound, shards=(), held_as=jnp.bfloat16):
    entries = jax.random.normal(stream_key, extent, jnp.float32) * deviation
    if len(shards) > 0:
        entries = steps_of(stream_key, extent, shards, -0.22, 0.18) * entries
    return jnp.clip(entries, min=-bound, max=bound).astype(held_as)


def noise_with(rng, shape, deviation, bound, cuts, heavy, kind=jnp.bfloat16):
    values = deviation * jax.random.normal(rng, shape, jnp.float32)
    if cuts:
        values = values * steps_of(rng, shape, cuts, -0.22, 0.18)
    return jnp.clip(strengthened(values, jax.random.fold_in(rng, 3), *heavy), -bound, bound).astype(kind)


def setup_inputs(seed: int = 0) -> dict:
    key_list = jax.random.split(jax.random.key(seed), 9)
    return {
        "coef_init": centred(key_list[0], (R, C), 1.0, 6.0, ((0, 32),), jnp.float32),
        "basis": noise_with(key_list[1], (ROWS, R), R ** -0.5, 0.375, ((0, 32),), (0, 1, 32, 2.75)),
        "basis_scale": jnp.clip(jnp.exp(math.log(2.0) - 1.3862944 * jax.random.uniform(key_list[2], (ROWS // TILE,), jnp.float32) ** steps_of(key_list[2], (ROWS // TILE,), ((0, 32),), -0.2, 0.2)), 0.5, 2.0),
        "ext_force": centred(key_list[3], (ROWS, C), 1.0, 6.0, ((0, 32),), jnp.float32),
        "precond": draw_precond(jax.random.fold_in(key_list[8], 71), 0),
        "connectivity": draw_connectivity(jax.random.fold_in(key_list[8], 71), 0),
        "halo_nodes": draw_halo_nodes(jax.random.fold_in(key_list[8], 71), 0),
        "plastic": plant((jax.random.randint(key_list[7], (ELEMS,), 0, 2) < 1).astype(jnp.int32), jax.random.fold_in(key_list[7], 1), 0, 1),
    }


STEP_SIZE = 0.5
SHEAR_MODULUS = 1.0
LAME_FIRST = 1.5
HARDENING = 0.5
YIELD_STRESS = 3.0
EPSILON = 1e-05

def corner_table():
    corner_bits = jnp.arange(8)[:, None] >> jnp.arange(3)[None, :] & 1
    return (2.0 * corner_bits.astype(jnp.float32) - 1.0) / 4.0

def element_forces(corner_disp, flags, corners):
    gradient = jnp.einsum('eaic,aj->eijc', corner_disp, corners, precision=lax.Precision.HIGHEST)
    strain = 0.5 * (gradient + jnp.swapaxes(gradient, 1, 2))
    volumetric = strain[:, 0, 0] + strain[:, 1, 1] + strain[:, 2, 2]
    identity = jnp.eye(3, dtype=jnp.float32)[None, :, :, None]
    shear_part = 2.0 * SHEAR_MODULUS * (strain - volumetric[:, None, None] / 3.0 * identity)
    magnitude = jnp.sqrt(lax.optimization_barrier(jnp.sum(shear_part * shear_part, axis=(1, 2))))
    total_modulus = 2.0 * SHEAR_MODULUS + HARDENING
    plastic_factor = HARDENING / total_modulus + 2.0 * SHEAR_MODULUS * YIELD_STRESS / (total_modulus * jnp.maximum(magnitude, YIELD_STRESS))
    factor = jnp.where(flags[:, None] == 1, plastic_factor, jnp.ones_like(plastic_factor))
    stress = LAME_FIRST * volumetric[:, None, None] * identity + factor[:, None, None] * shear_part
    return jnp.einsum('eijc,aj->eaic', stress, corners, precision=lax.Precision.HIGHEST)

def apply_scale(values, scales):
    return (values.reshape(scales.shape[0], -1, values.shape[-1]) * scales[:, None, None]).reshape(values.shape)

def reference(coef_init, basis, basis_scale, ext_force, precond, connectivity, halo_nodes, plastic):
    corners = corner_table()
    cases = coef_init.shape[1]
    element_device = (jnp.arange(ELEMS) // ELEM_DEV).astype(jnp.int32)[:, None]
    halo_padded = jnp.concatenate([halo_nodes, jnp.zeros((HALO,), jnp.int32)])
    halo_slot = jnp.clip(connectivity - NODE_DEV, 0, HALO - 1).astype(jnp.int32)
    neighbour = element_device + 1
    halo_target = neighbour * NODE_DEV + halo_padded[(neighbour * HALO + halo_slot).astype(jnp.int32)]
    global_index = jnp.where(connectivity < NODE_DEV, element_device * NODE_DEV + connectivity, halo_target).astype(jnp.int32)
    blocks = (global_index.reshape(N_DOM, ELEM_DEV, 8), plastic.reshape(N_DOM, ELEM_DEV))
    coefficients = coef_init
    nodal_residual = ext_force
    for sweep in range(ITERS):
        coef_low = coefficients.astype(jnp.bfloat16)
        displacement = apply_scale(jnp.dot(basis, coef_low, preferred_element_type=jnp.float32), basis_scale)
        nodes = jnp.concatenate([displacement.reshape(NODES, 3, cases), jnp.zeros((NODE_DEV, 3, cases), jnp.float32)])

        def accumulate(internal, inputs):
            block_index, flags = inputs
            corner_force = element_forces(nodes[block_index], flags, corners)
            return (internal.at[block_index.reshape(-1)].add(corner_force.reshape(-1, 3, cases)), None)
        internal, unused = lax.scan(accumulate, jnp.zeros((NODES + NODE_DEV, 3, cases), jnp.float32), blocks)
        nodal_residual = ext_force - internal[:NODES].reshape(ROWS, cases)
        scaled = apply_scale(nodal_residual, basis_scale).astype(jnp.bfloat16)
        reduced = lax.dot_general(basis, scaled, (((0,), (0,)), ((), ())), preferred_element_type=jnp.float32)
        update = precond[:, None] * reduced
        root_mean = jnp.sqrt(lax.optimization_barrier(jnp.mean(update * update, axis=0)) + EPSILON)
        coefficients = coefficients + STEP_SIZE * update / root_mean
    return (coefficients, nodal_residual)
```

```python
import functools
import math

import jax
import jax.numpy as jnp
from jax import lax
from jax.experimental import pallas as pl
from jax.experimental.pallas import tpu as pltpu
from jax.sharding import PartitionSpec as P

STEP_SIZE = 0.5
SHEAR_MODULUS = 1.0
LAME_FIRST = 1.5
HARDENING = 0.5
YIELD_STRESS = 3.0
EPSILON = 1e-05
ITERS = 2
LANES = 128
SUB = 8
F32 = jnp.float32
BF16 = jnp.bfloat16


def grid_of(node_count, halo_count, elem_count):
    layers = node_count // halo_count
    assert layers == 2
    total = halo_count + 1 - elem_count // layers
    root = math.isqrt(total * total - 4 * halo_count)
    gx = (total + root) // 2
    gy = halo_count // gx
    assert gx * gy == halo_count and (gx - 1) * (gy - 1) * layers == elem_count
    assert gx == gy and gy % SUB == 0
    return gx, gy


def grid_index(p, gx, gy):
    nb = gy // SUB
    q, s = p // SUB, p % SUB
    return (nb * s + q // gx) * gx + q % gx


def column_of(row):
    n = row.shape[1]
    eye = lax.broadcasted_iota(jnp.int32, (n, n), 0) == lax.broadcasted_iota(jnp.int32, (n, n), 1)
    return jnp.sum(jnp.where(eye, row, 0.0), axis=1, keepdims=True)


def row_of(col):
    n = col.shape[0]
    eye = lax.broadcasted_iota(jnp.int32, (n, n), 0) == lax.broadcasted_iota(jnp.int32, (n, n), 1)
    return jnp.sum(jnp.where(eye, col, 0.0), axis=0, keepdims=True)


def split2(value):
    high = value.astype(BF16).astype(F32)
    return high, value - high


def first_layer_column(halo_row, gx, gy):
    n = gx * gy
    want = grid_index(lax.broadcasted_iota(jnp.int32, (n, n), 0), gx, gy)
    hit = lax.broadcasted_iota(jnp.int32, (n, n), 1) == want
    return jnp.sum(jnp.where(hit, halo_row, 0.0), axis=1, keepdims=True)


def select_rows(node_col, i, rows):
    n = node_col.shape[0]
    pick = (3.0 * node_col + i).astype(jnp.int32)
    return jnp.where(lax.broadcasted_iota(jnp.int32, (n, rows), 1) == pick, 1.0, 0.0).astype(BF16)


def scale_block(node_col, i, scale_row, tile):
    n, tiles = node_col.shape[0], scale_row.shape[1]
    row = 3.0 * node_col + i
    low = lax.broadcasted_iota(jnp.int32, (n, tiles), 1).astype(F32) * tile
    scale = jnp.sum(jnp.where((row >= low) & (row < low + tile), scale_row, 0.0), axis=1, keepdims=True)
    high, rest = split2(scale)
    middle, last = split2(rest)
    lane = lax.broadcasted_iota(jnp.int32, (n, LANES), 1)
    return jnp.where(lane == 0, high, jnp.where(lane == 1, middle, jnp.where(lane == 2, last, 0.0))).astype(BF16)


def spread_kernel(parts, coef_ref, precond_ref, out_ref):
    owned, cases = coef_ref.shape
    per, spans = cases // parts, LANES // owned
    high, low = split2(coef_ref[...])
    out_ref[:, :owned, :] = jnp.broadcast_to(high.astype(BF16)[None], (parts, owned, cases))
    mine = lax.rem(lax.axis_index("dom"), spans)
    lane = lax.broadcasted_iota(jnp.int32, (1, LANES), 1) // owned
    low = jnp.concatenate([low] * spans, axis=0).T
    low = jnp.where(lane == mine, low, 0.0).astype(BF16)
    rest = jnp.dot(unfold_matrix(parts, per, 0).T.astype(BF16), low, preferred_element_type=F32)
    scale = jnp.where(lane == mine, jnp.concatenate([precond_ref[...]] * spans, axis=1), 0.0)
    first, scale = split2(scale)
    second, third = split2(scale)
    row = lax.rem(lax.broadcasted_iota(jnp.int32, (parts * SUB, LANES), 0), SUB) - per
    rest = rest + jnp.where(row == 0, first, jnp.where(row == 1, second, jnp.where(row == 2, third, 0.0)))
    out_ref[:, owned:, :] = rest.reshape(parts, SUB, LANES).astype(BF16)


def unfold_matrix(parts, per, half):
    cases = parts * per
    c = lax.broadcasted_iota(jnp.int32, (cases, parts * SUB), 0)
    row = lax.broadcasted_iota(jnp.int32, (cases, parts * SUB), 1)
    return jnp.where(row == (c // per) * SUB + lax.rem(c, per) + half * per, 1.0, 0.0)


def setup_kernel(
    gx, gy, tile, halo_ref, scale_ref, conn_ref, plastic_ref, ext_ref, basis_ref,
    out_ref, ext_out_ref, flag_ref, flag_row_ref, node_ref, pick_ref,
):
    n = gx * gy
    rows, rank = basis_ref.shape
    conn = conn_ref[...].astype(F32)
    elems = conn.shape[1]
    place = grid_index(lax.broadcasted_iota(jnp.int32, (n, elems), 0), gx, gy).astype(F32) + 2 * n
    node0 = first_layer_column(halo_ref[...].astype(F32), gx, gy)
    node1 = jnp.full((n, 1), -1.0, F32)
    for corner in range(4):
        hit = conn[4 + corner : 5 + corner, :] == place
        found = jnp.max(jnp.where(hit, conn[corner : corner + 1, :], -1.0), axis=1, keepdims=True)
        node1 = jnp.maximum(node1, found)
    node_ref[...] = jnp.concatenate([row_of(node0), row_of(node1)], axis=1)
    active = (plastic_ref[...] == 1).astype(F32)
    cells = (conn[0:1, :] == jnp.broadcast_to(node0, (n, elems)), conn[4:5, :] == place)
    for layer, hit in enumerate(cells):
        flag = jnp.max(jnp.where(hit, active, 0.0), axis=1, keepdims=True)
        flag_ref[layer] = jnp.broadcast_to(flag, (n, LANES))
    flag_row_ref[...] = jnp.zeros_like(flag_row_ref)
    flag = row_of(flag)
    for row in range(n // LANES):
        flag_row_ref[row : row + 1, :] = flag[:, row * LANES : (row + 1) * LANES]
    for layer, node in enumerate((node0, node1)):
        for i in range(3):
            start = (3 * layer + i) * n
            pick_ref[start : start + n, :] = select_rows(node, i, rows)
            out_ref[start : start + n, rank:] = scale_block(node, i, scale_ref[...], tile)
    high, low = split2(ext_ref[...])
    cases = ext_ref.shape[1]
    loads = jnp.concatenate([high.astype(BF16), low.astype(BF16)], axis=1)
    for block in range(6):
        start = block * n
        pick = pick_ref[start : start + n, :]
        both = jnp.dot(pick, loads, preferred_element_type=F32)
        ext_out_ref[start : start + n, :] = both[:, :cases] + both[:, cases:]
        out_ref[start : start + n, :rank] = jnp.dot(
            pick, basis_ref[...], preferred_element_type=F32
        ).astype(BF16)


def cell_forces(gx, nb, flag_ref, below, above, add_below, add_above):
    quarter = 0.25
    n = gx * nb * SUB

    def load(ref, first, x, yb):
        start = first + (yb * gx + x) * SUB
        return ref[start : start + SUB, :]

    def level(x):
        total, jump = [], []
        for i in range(3):
            low = [load(below[0], below[1] + i * n, x, yb) for yb in range(nb)]
            high = [load(above[0], above[1] + i * n, x, yb) for yb in range(nb)]
            total.append([a + b for a, b in zip(low, high)])
            jump.append([b - a for a, b in zip(low, high)])
        return total, jump

    def roll_up(v):
        return pltpu.roll(v, SUB - 1, 0)

    def roll_down(v):
        return pltpu.roll(v, 1, 0)

    inside = lax.broadcasted_iota(jnp.int32, (SUB, LANES), 0) < SUB - 1
    total_modulus = 2.0 * SHEAR_MODULUS + HARDENING
    here = level(0)
    carry = None
    for x in range(gx - 1):
        there = level(x + 1)
        grad = [[[None] * 3 for _ in range(3)] for _ in range(nb)]
        for i in range(3):
            sum_x = [a + b for a, b in zip(here[0][i], there[0][i])]
            dif_x = [b - a for a, b in zip(here[0][i], there[0][i])]
            jmp_x = [a + b for a, b in zip(here[1][i], there[1][i])]
            sum_n = sum_x[1:] + [roll_up(sum_x[0])]
            dif_n = dif_x[1:] + [roll_up(dif_x[0])]
            jmp_n = jmp_x[1:] + [roll_up(jmp_x[0])]
            for yb in range(nb):
                grad[yb][i][0] = dif_x[yb] + dif_n[yb]
                grad[yb][i][1] = sum_n[yb] - sum_x[yb]
                grad[yb][i][2] = jmp_x[yb] + jmp_n[yb]
        stress = []
        for yb in range(nb):
            g = grad[yb]
            vol = (g[0][0] + g[1][1] + g[2][2]) * quarter
            third = vol * (2.0 * SHEAR_MODULUS / 3.0)
            diag = [g[i][i] * (2.0 * SHEAR_MODULUS * quarter) - third for i in range(3)]
            off = [
                (g[i][j] + g[j][i]) * (SHEAR_MODULUS * quarter) for i, j in ((0, 1), (0, 2), (1, 2))
            ]
            norm = diag[0] * diag[0] + diag[1] * diag[1] + diag[2] * diag[2]
            norm = norm + 2.0 * (off[0] * off[0] + off[1] * off[1] + off[2] * off[2])
            ratio = YIELD_STRESS * lax.rsqrt(jnp.maximum(norm, YIELD_STRESS * YIELD_STRESS))
            soft = HARDENING / total_modulus + (2.0 * SHEAR_MODULUS / total_modulus) * ratio
            factor = jnp.where(load(flag_ref, 0, x, yb) > 0.5, soft, 1.0)
            mean = LAME_FIRST * vol
            s = [None] * 6
            for i in range(3):
                s[i] = (mean + factor * diag[i]) * quarter
                s[3 + i] = factor * off[i] * quarter
            if yb == nb - 1:
                s = [jnp.where(inside, v, 0.0) for v in s]
            stress.append([[s[0], s[3], s[4]], [s[3], s[1], s[5]], [s[4], s[5], s[2]]])
        new_carry = []
        for i in range(3):
            ax = [stress[yb][i][0] for yb in range(nb)]
            ay = [stress[yb][i][1] for yb in range(nb)]
            az = [stress[yb][i][2] for yb in range(nb)]
            ax_p = [roll_down(ax[-1])] + ax[:-1]
            ay_p = [roll_down(ay[-1])] + ay[:-1]
            az_p = [roll_down(az[-1])] + az[:-1]
            for yb in range(nb):
                fx = ax_p[yb] + ax[yb]
                fy = ay_p[yb] - ay[yb]
                fz = az_p[yb] + az[yb]
                back, front = fy - fx, fy + fx
                low, high = back - fz, back + fz
                if carry is not None:
                    low, high = low + carry[i * nb + yb][0], high + carry[i * nb + yb][1]
                if add_below is not None:
                    add_below(i, x, yb, low)
                if add_above is not None:
                    add_above(i, x, yb, high)
                new_carry.append((front - fz, front + fz))
        carry = new_carry
        here = there
    for i in range(3):
        for yb in range(nb):
            if add_below is not None:
                add_below(i, gx - 1, yb, carry[i * nb + yb][0])
            if add_above is not None:
                add_above(i, gx - 1, yb, carry[i * nb + yb][1])


def scale_of(ref, cases):
    rank = ref.shape[1] - LANES
    return jnp.dot(ref[:, rank:], jnp.ones((LANES, cases), BF16), preferred_element_type=F32)


def times_transposed(a, b):
    return lax.dot_general(a, b, (((1,), (1,)), ((), ())), preferred_element_type=F32)


def lift_kernel(folded, coef_ref, basis_ref, flag_row_ref, disp_ref, near_ref, far_ref):
    rank = basis_ref.shape[1] - LANES
    if folded:
        parts, _, half = coef_ref.shape
        coef = coef_ref[...].reshape(parts * SUB, half)
        per = rank // half * SUB // 4
        per = SUB * half // rank
        lifted = None
        for part in range(2):
            turn = unfold_matrix(parts, per, part).astype(BF16)
            block = jnp.dot(turn, coef, preferred_element_type=F32).astype(BF16)
            term = times_transposed(basis_ref[:, part * half : (part + 1) * half], block)
            lifted = term if lifted is None else lifted + term
    else:
        coef = coef_ref[...] if coef_ref.ndim == 2 else coef_ref[:, : coef_ref.shape[1] - SUB, :]
        lifted = jnp.dot(basis_ref[:, :rank], coef.reshape(rank, -1), preferred_element_type=F32)
    disp_ref[...] = lifted * scale_of(basis_ref, lifted.shape[1])
    layer = disp_ref.shape[0] // 2
    odd = lax.rem(lax.axis_index("dom"), 2)
    near_ref[:layer, :] = disp_ref[pl.ds(pl.multiple_of((1 - odd) * layer, layer), layer), :].astype(BF16)
    far_ref[:layer, :] = disp_ref[pl.ds(pl.multiple_of(odd * layer, layer), layer), :].astype(BF16)
    near_ref[layer:, :] = flag_row_ref[...].astype(BF16)
    far_ref[layer:, :] = flag_row_ref[...].astype(BF16)


def putter(gx, n, f_ref, layer, source=None, live=None):
    def put(i, x, yb, value):
        start = (3 * layer + i) * n + (yb * gx + x) * SUB
        if live is not None:
            value = jnp.where(live, value, 0.0)
        if source is not None:
            value = source[start : start + SUB, :] + value
        f_ref[start : start + SUB, :] = value

    return put


def own_kernel(gx, gy, disp_ref, flag_ref, force_ref):
    n, nb = gx * gy, gy // SUB
    put = functools.partial(putter, gx, n, force_ref)
    cell_forces(gx, nb, flag_ref.at[0], (disp_ref, 0), (disp_ref, 3 * n), put(0), put(1))


def sweep_kernel(
    gx, gy, folded, disp_ref, force_ref, near_ref, far_ref, basis_ref, ext_ref, flag_ref,
    part_ref, resid_ref, side_ref, side_flag_ref, scaled_ref,
):
    n, nb = gx * gy, gy // SUB
    layer = 3 * n
    rank = basis_ref.shape[1] - LANES
    me = lax.axis_index("dom")
    even = lax.rem(me, 2) == 0
    near, far = near_ref[...].astype(F32), far_ref[...].astype(F32)
    side_ref[:layer, :] = jnp.where(even, far[:layer, :], near[:layer, :])
    side_ref[layer:, :] = jnp.where(even, near[:layer, :], far[:layer, :])
    flags = jnp.where(even, far[layer:, :], near[layer:, :])
    for row in range(n // LANES):
        flag = column_of(flags[row : row + 1, :])
        side_flag_ref[row * LANES : (row + 1) * LANES, :] = jnp.broadcast_to(flag, (LANES, LANES))
    put = functools.partial(putter, gx, n, resid_ref)
    live = jnp.broadcast_to(me > 0, (SUB, LANES))
    cell_forces(
        gx, nb, side_flag_ref, (side_ref, 0), (disp_ref, 0), None, put(0, force_ref, live)
    )
    cell_forces(
        gx, nb, flag_ref.at[1], (disp_ref, layer), (side_ref, layer), put(1, force_ref), None
    )
    resid = ext_ref[...] - resid_ref[...]
    resid_ref[...] = resid
    scaled_ref[...] = (resid * scale_of(basis_ref, resid.shape[1])).astype(BF16)
    if folded:
        parts, _, half = part_ref.shape
        per = SUB * half // rank
        total = None
        for part in range(2):
            turn = unfold_matrix(parts, per, part).T.astype(BF16)
            block = times_transposed(turn, scaled_ref[...]).astype(BF16)
            term = jnp.dot(block, basis_ref[:, part * half : (part + 1) * half], preferred_element_type=F32)
            total = term if total is None else total + term
        part_ref[...] = total.reshape(part_ref.shape).astype(BF16)
    else:
        part_ref[...] = jnp.dot(scaled_ref[...].astype(F32).T.astype(BF16), basis_ref[:, :rank], preferred_element_type=F32)


def fold(value):
    half = value.shape[1] // 2
    row = lax.broadcasted_iota(jnp.int32, (SUB, half), 0)
    return jnp.where(row < SUB // 2, value[:, :half], pltpu.roll(value[:, half:], SUB // 2, 0))


def step(coef, update, rank):
    square = jnp.broadcast_to(jnp.sum(update * update, axis=1, keepdims=True), (SUB, LANES))
    square = (square + pltpu.roll(square, SUB // 2, 0))[:, 0:1]
    return coef + STEP_SIZE * update * lax.rsqrt(square / rank + EPSILON)


def middle_kernel(rank, parts_ref, start_ref, coef_ref, scale_ref, send_ref):
    parts, depth, cases = start_ref.shape
    owned, per, spans = depth - SUB, cases // parts, LANES * parts // rank
    me = lax.axis_index("dom")
    rest = start_ref[:, owned:, :].astype(F32)
    rest = [jnp.sum(rest[k * spans : (k + 1) * spans], axis=0) for k in range(parts // spans)]
    rest = jnp.concatenate(rest, axis=1)
    pick = lax.broadcasted_iota(jnp.int32, (SUB, cases), 0)
    lane = lax.broadcasted_iota(jnp.int32, (SUB, cases), 1)
    pick = jnp.where((lane == pick + me * per) & (pick < per), 1.0, 0.0).astype(BF16)
    high = times_transposed(pick, start_ref[:, :owned, :].reshape(rank, cases))
    scale = jnp.sum(rest[per : per + 3, :], axis=0, keepdims=True)
    scale = fold(jnp.broadcast_to(scale, (SUB, rank)))
    scale_ref[...] = scale
    update = scale * jnp.sum(parts_ref[...].astype(F32), axis=0)
    coef = step(fold(high + rest), update, rank)
    coef_ref[...] = coef
    send_ref[...] = jnp.broadcast_to(coef.astype(BF16)[None], send_ref.shape)


def last_kernel(rank, owned, parts_ref, coef_ref, scale_ref, send_ref):
    update = scale_ref[...] * jnp.sum(parts_ref[...].astype(F32), axis=0)
    coef = step(coef_ref[...], update, rank)
    parts, spans = send_ref.shape[0], LANES // owned
    for device in range(parts):
        block = device % (parts // 2) // spans
        send_ref[device] = coef[:, block * LANES : (block + 1) * LANES]


def finish_kernel(got_ref, out_ref, turned_ref):
    owned, cases = out_ref.shape
    parts = got_ref.shape[0]
    per, spans = cases // parts, LANES // owned
    me = lax.axis_index("dom")
    high, rest = split2(got_ref[...].reshape(parts * SUB, LANES))
    middle, low = split2(rest)
    turn = jnp.where(me < parts // 2, unfold_matrix(parts, per, 0), unfold_matrix(parts, per, 1)).astype(BF16)
    total = None
    for value in (high, middle, low):
        term = jnp.dot(turn, value.astype(BF16), preferred_element_type=F32)
        total = term if total is None else total + term
    turned_ref[...] = total.T
    first = pl.multiple_of(lax.rem(me, spans) * owned, owned)
    out_ref[...] = turned_ref[pl.ds(first, owned), :]


def unpermute_kernel(gx, gy, node_ref, resid_ref, out_ref, parts_ref):
    n = gx * gy
    rows, cases = resid_ref.shape
    high, low = split2(resid_ref[...])
    parts_ref[:, :cases] = high.astype(BF16)
    parts_ref[:, cases:] = low.astype(BF16)
    node = node_ref[...]
    target = jnp.concatenate(
        [3.0 * node[:, layer * n : (layer + 1) * n] + i for layer in range(2) for i in range(3)], axis=1
    ).astype(jnp.int32)
    step = rows // 3
    for start in range(0, rows, step):
        here = lax.broadcasted_iota(jnp.int32, (step, rows), 0) + start
        pick = jnp.where(here == target, 1.0, 0.0).astype(BF16)
        both = jnp.dot(pick, parts_ref[...], preferred_element_type=F32)
        out_ref[start : start + step, :] = both[:, :cases] + both[:, cases:]


def call(kernel, name, outs, scratch=(), vmem=24, flops=0, nbytes=0):
    return pl.pallas_call(
        kernel,
        name=name,
        out_shape=outs,
        scratch_shapes=list(scratch),
        compiler_params=pltpu.CompilerParams(vmem_limit_bytes=vmem << 20),
        cost_estimate=pl.CostEstimate(flops=flops, bytes_accessed=nbytes, transcendentals=0),
    )


def on_device(coef_init, basis, basis_scale, ext_force, precond, connectivity, halo_nodes, plastic):
    parts = lax.axis_size("dom")
    rows, cases = ext_force.shape
    rank = basis.shape[1]
    owned = coef_init.shape[0]
    n = halo_nodes.shape[0]
    elems = connectivity.shape[0]
    gx, gy = grid_of(rows // 3, n, elems)
    tile = rows // basis_scale.shape[0]
    half = rank // 2
    layer = 3 * n
    folded = parts * (SUB // 2) == cases and LANES % owned == 0
    shape = jax.ShapeDtypeStruct

    def exchange(value):
        return lax.all_to_all(value, "dom", 0, 0)

    if folded:
        start = exchange(
            call(functools.partial(spread_kernel, parts), "spread", shape((parts, owned + SUB, cases), BF16))(
                coef_init, precond.reshape(1, owned)
            )
        )
    else:
        coef = lax.all_gather(coef_init, "dom", axis=0, tiled=True)
        scaling = lax.all_gather(precond, "dom", axis=0, tiled=True)
    basis_grid, ext_grid, flags, flag_row, nodes = call(
        functools.partial(setup_kernel, gx, gy, tile),
        "setup",
        (
            shape((rows, rank + LANES), BF16),
            shape((rows, cases), F32),
            shape((2, n, LANES), F32),
            shape((SUB, LANES), F32),
            shape((1, 2 * n), F32),
        ),
        [pltpu.VMEM((rows, rows), BF16)],
        flops=2 * rows * rows * (rank + 2 * cases),
        nbytes=4 * rows * rank,
    )(
        halo_nodes.reshape(1, n),
        basis_scale.reshape(1, -1),
        connectivity.T,
        plastic.reshape(1, elems),
        ext_force,
        basis,
    )
    near_pairs = [(d, d ^ 1) for d in range(parts)]
    far_pairs = [pair for d in range(1, parts - 1, 2) for pair in ((d, d + 1), (d + 1, d))]
    for sweep in range(ITERS):
        second = folded and sweep > 0
        source = (send if second else start) if folded else coef.astype(BF16)
        side = shape((layer + SUB, cases), BF16)
        disp, near, far = call(
            functools.partial(lift_kernel, second),
            "lift",
            (shape((rows, cases), F32), side, side),
            flops=2 * rows * rank * cases,
        )(source, basis_grid, flag_row)
        far = lax.ppermute(far, "dom", far_pairs)
        near = lax.ppermute(near, "dom", near_pairs)
        force = call(
            functools.partial(own_kernel, gx, gy),
            "own",
            shape((rows, cases), F32),
            flops=rows * rank * cases,
        )(disp, flags)
        part, resid = call(
            functools.partial(sweep_kernel, gx, gy, folded),
            "sweep",
            (
                shape((parts, SUB, half), BF16) if folded else shape((cases, rank), F32),
                shape((rows, cases), F32),
            ),
            [
                pltpu.VMEM((2 * layer, cases), F32),
                pltpu.VMEM((n, LANES), F32),
                pltpu.VMEM((rows, cases), BF16),
            ],
            flops=4 * rows * rank * cases,
        )(disp, force, near, far, basis_grid, ext_grid, flags)
        if folded:
            part = exchange(part)
            if sweep < ITERS - 1:
                mid = shape((SUB, half), F32)
                if sweep == 0:
                    mine, scaling, send = call(
                        functools.partial(middle_kernel, rank), "middle", (mid, mid, shape(part.shape, BF16))
                    )(part, start)
                send = exchange(send)
        else:
            update = scaling[:, None] * lax.psum(part, "dom").T
            root = jnp.sqrt(jnp.sum(update * update, axis=0) / rank + EPSILON)
            coef = coef + STEP_SIZE * update / root
    nodal_residual = call(
        functools.partial(unpermute_kernel, gx, gy),
        "unpermute",
        shape((rows, cases), F32),
        [pltpu.VMEM((rows, 2 * cases), BF16)],
        flops=2 * rows * rows * 2 * cases,
    )(nodes, resid)
    if folded:
        cut = call(functools.partial(last_kernel, rank, owned), "last", shape((parts, SUB, LANES), F32))(
            part, mine, scaling
        )
        coef_out = call(finish_kernel, "finish", shape((owned, cases), F32), [pltpu.VMEM((LANES, cases), F32)])(
            exchange(cut)
        )
    else:
        coef_out = lax.dynamic_slice_in_dim(coef, lax.axis_index("dom") * owned, owned, 0)
    return coef_out, nodal_residual


def solution(mesh):
    return jax.shard_map(
        on_device,
        mesh=mesh,
        in_specs=(
            P("dom", None),
            P("dom", None),
            P("dom"),
            P("dom", None),
            P("dom"),
            P("dom", None),
            P("dom"),
            P("dom"),
        ),
        out_specs=(P("dom", None), P("dom", None)),
        check_vma=False,
    )
```

```python
import functools
import math

import jax
import jax.numpy as jnp
from jax import lax
from jax.experimental import pallas as pl
from jax.experimental.pallas import tpu as pltpu
from jax.sharding import PartitionSpec as P

STEP_SIZE = 0.5
SHEAR_MODULUS = 1.0
LAME_FIRST = 1.5
HARDENING = 0.5
YIELD_STRESS = 3.0
EPSILON = 1e-05
ITERS = 2
LANES = 128
SUB = 8
F32 = jnp.float32
BF16 = jnp.bfloat16


def grid_of(node_count, halo_count, elem_count):
    layers = node_count // halo_count
    assert layers == 2
    total = halo_count + 1 - elem_count // layers
    root = math.isqrt(total * total - 4 * halo_count)
    gx = (total + root) // 2
    gy = halo_count // gx
    assert gx * gy == halo_count and (gx - 1) * (gy - 1) * layers == elem_count
    assert gx == gy and gy % SUB == 0
    return gx, gy


def grid_index(p, gx, gy):
    nb = gy // SUB
    q, s = p // SUB, p % SUB
    return (nb * s + q // gx) * gx + q % gx


def column_of(row):
    n = row.shape[1]
    eye = lax.broadcasted_iota(jnp.int32, (n, n), 0) == lax.broadcasted_iota(jnp.int32, (n, n), 1)
    return jnp.sum(jnp.where(eye, row, 0.0), axis=1, keepdims=True)


def row_of(col):
    n = col.shape[0]
    eye = lax.broadcasted_iota(jnp.int32, (n, n), 0) == lax.broadcasted_iota(jnp.int32, (n, n), 1)
    return jnp.sum(jnp.where(eye, col, 0.0), axis=0, keepdims=True)


def split2(value):
    high = value.astype(BF16).astype(F32)
    return high, value - high


def first_layer_column(halo_row, gx, gy):
    n = gx * gy
    want = grid_index(lax.broadcasted_iota(jnp.int32, (n, n), 0), gx, gy)
    hit = lax.broadcasted_iota(jnp.int32, (n, n), 1) == want
    return jnp.sum(jnp.where(hit, halo_row, 0.0), axis=1, keepdims=True)


def select_rows(node_col, i, rows):
    n = node_col.shape[0]
    pick = (3.0 * node_col + i).astype(jnp.int32)
    return jnp.where(lax.broadcasted_iota(jnp.int32, (n, rows), 1) == pick, 1.0, 0.0).astype(BF16)


def scale_block(node_col, i, scale_row, tile, flag):
    n, tiles = node_col.shape[0], scale_row.shape[1]
    row = 3.0 * node_col + i
    low = lax.broadcasted_iota(jnp.int32, (n, tiles), 1).astype(F32) * tile
    scale = jnp.sum(jnp.where((row >= low) & (row < low + tile), scale_row, 0.0), axis=1, keepdims=True)
    high, rest = split2(scale)
    middle, last = split2(rest)
    lane = lax.broadcasted_iota(jnp.int32, (n, LANES), 1)
    return jnp.where(lane == 0, high, jnp.where(lane == 1, middle, jnp.where(lane == 2, last, jnp.where(lane == 3, flag, 0.0)))).astype(BF16)


def start_copies(sources, targets, sems):
    copies = [pltpu.make_async_copy(a, b, sems.at[i]) for i, (a, b) in enumerate(zip(sources, targets))]
    for copy in copies:
        copy.start()
    return copies


def spread_kernel(parts, coef_hbm, precond_hbm, out_ref, coef_ref, precond_ref, sems):
    owned, cases = coef_ref.shape
    per, spans = cases // parts, LANES // owned
    for copy in start_copies((coef_hbm, precond_hbm), (coef_ref, precond_ref), sems):
        copy.wait()
    high, low = split2(coef_ref[...])
    out_ref[:, :owned, :] = jnp.broadcast_to(high.astype(BF16)[None], (parts, owned, cases))
    mine = lax.rem(lax.axis_index("dom"), spans)
    lane = lax.broadcasted_iota(jnp.int32, (1, LANES), 1) // owned
    low = jnp.concatenate([low] * spans, axis=0).T
    low = jnp.where(lane == mine, low, 0.0).astype(BF16)
    rest = jnp.dot(unfold_matrix(parts, per, 0).T.astype(BF16), low, preferred_element_type=F32)
    scale = jnp.where(lane == mine, jnp.concatenate([precond_ref[...]] * spans, axis=1), 0.0)
    first, scale = split2(scale)
    second, third = split2(scale)
    row = lax.rem(lax.broadcasted_iota(jnp.int32, (parts * SUB, LANES), 0), SUB) - per
    rest = rest + jnp.where(row == 0, first, jnp.where(row == 1, second, jnp.where(row == 2, third, 0.0)))
    out_ref[:, owned:, :] = rest.reshape(parts, SUB, LANES).astype(BF16)


def unfold_matrix(parts, per, half):
    cases = parts * per
    c = lax.broadcasted_iota(jnp.int32, (cases, parts * SUB), 0)
    row = lax.broadcasted_iota(jnp.int32, (cases, parts * SUB), 1)
    return jnp.where(row == (c // per) * SUB + lax.rem(c, per) + half * per, 1.0, 0.0)


def setup_kernel(
    gx, gy, tile, halo_hbm, scale_hbm, conn_hbm, plastic_hbm, ext_hbm, basis_hbm,
    out_ref, ext_out, flag_row_ref, node_ref,
    ext_grid_ref, out_sems, halo_ref, scale_ref, conn_ref, plastic_ref, ext_ref, basis_ref, sems,
):
    n = gx * gy
    rows, rank = basis_ref.shape
    copies = start_copies(
        (halo_hbm, scale_hbm, conn_hbm, plastic_hbm, ext_hbm, basis_hbm),
        (halo_ref, scale_ref, conn_ref, plastic_ref, ext_ref, basis_ref),
        sems,
    )
    for copy in copies[:4]:
        copy.wait()
    conn = conn_ref[...].astype(F32)
    elems = conn.shape[1]
    place = grid_index(lax.broadcasted_iota(jnp.int32, (n, elems), 0), gx, gy).astype(F32) + 2 * n
    node0 = first_layer_column(halo_ref[...].astype(F32), gx, gy)
    node1 = jnp.full((n, 1), -1.0, F32)
    for corner in range(4):
        hit = conn[4 + corner : 5 + corner, :] == place
        found = jnp.max(jnp.where(hit, conn[corner : corner + 1, :], -1.0), axis=1, keepdims=True)
        node1 = jnp.maximum(node1, found)
    active = (plastic_ref[...] == 1).astype(F32)
    cells = (conn[0:1, :] == jnp.broadcast_to(node0, (n, elems)), conn[4:5, :] == place)
    flags = [jnp.max(jnp.where(hit, active, 0.0), axis=1, keepdims=True) for hit in cells]
    flag_row_ref[...] = jnp.zeros_like(flag_row_ref)
    flag = row_of(flags[1])
    for row in range(n // LANES):
        flag_row_ref[row : row + 1, :] = flag[:, row * LANES : (row + 1) * LANES]
    node_ref[...] = jnp.concatenate([row_of(node0), row_of(node1)], axis=1)
    copies[4].wait()
    high, low = split2(ext_ref[...])
    cases = ext_ref.shape[1]
    loads = jnp.concatenate([high.astype(BF16), low.astype(BF16)], axis=1)
    copies[5].wait()
    for layer, node in enumerate((node0, node1)):
        for i in range(3):
            start = (3 * layer + i) * n
            pick = select_rows(node, i, rows)
            both = jnp.dot(pick, loads, preferred_element_type=F32)
            ext_grid_ref[start : start + n, :] = both[:, :cases] + both[:, cases:]
            out_ref[start : start + n, rank:] = scale_block(node, i, scale_ref[...], tile, flags[layer])
            out_ref[start : start + n, :rank] = jnp.dot(
                pick, basis_ref[...], preferred_element_type=F32
            ).astype(BF16)
        if layer == 1:
            for copy in start_copies((ext_grid_ref,), (ext_out,), out_sems):
                copy.wait()


def cell_forces(gx, nb, flag_ref, below, above, add_below, add_above):
    quarter = 0.25
    n = gx * nb * SUB

    def load(ref, first, x, yb):
        start = first + (yb * gx + x) * SUB
        return ref[start : start + SUB, :]

    def level(x):
        total, jump = [], []
        for i in range(3):
            low = [load(below[0], below[1] + i * n, x, yb) for yb in range(nb)]
            high = [load(above[0], above[1] + i * n, x, yb) for yb in range(nb)]
            total.append([a + b for a, b in zip(low, high)])
            jump.append([b - a for a, b in zip(low, high)])
        return total, jump

    def roll_up(v):
        return pltpu.roll(v, SUB - 1, 0)

    def roll_down(v):
        return pltpu.roll(v, 1, 0)

    inside = lax.broadcasted_iota(jnp.int32, (SUB, LANES), 0) < SUB - 1
    total_modulus = 2.0 * SHEAR_MODULUS + HARDENING
    here = level(0)
    carry = None
    for x in range(gx - 1):
        there = level(x + 1)
        grad = [[[None] * 3 for _ in range(3)] for _ in range(nb)]
        for i in range(3):
            sum_x = [a + b for a, b in zip(here[0][i], there[0][i])]
            dif_x = [b - a for a, b in zip(here[0][i], there[0][i])]
            jmp_x = [a + b for a, b in zip(here[1][i], there[1][i])]
            sum_n = sum_x[1:] + [roll_up(sum_x[0])]
            dif_n = dif_x[1:] + [roll_up(dif_x[0])]
            jmp_n = jmp_x[1:] + [roll_up(jmp_x[0])]
            for yb in range(nb):
                grad[yb][i][0] = dif_x[yb] + dif_n[yb]
                grad[yb][i][1] = sum_n[yb] - sum_x[yb]
                grad[yb][i][2] = jmp_x[yb] + jmp_n[yb]
        stress = []
        for yb in range(nb):
            g = grad[yb]
            vol = (g[0][0] + g[1][1] + g[2][2]) * quarter
            third = vol * (2.0 * SHEAR_MODULUS / 3.0)
            diag = [g[i][i] * (2.0 * SHEAR_MODULUS * quarter) - third for i in range(3)]
            off = [
                (g[i][j] + g[j][i]) * (SHEAR_MODULUS * quarter) for i, j in ((0, 1), (0, 2), (1, 2))
            ]
            norm = diag[0] * diag[0] + diag[1] * diag[1] + diag[2] * diag[2]
            norm = norm + 2.0 * (off[0] * off[0] + off[1] * off[1] + off[2] * off[2])
            ratio = YIELD_STRESS * lax.rsqrt(jnp.maximum(norm, YIELD_STRESS * YIELD_STRESS))
            soft = HARDENING / total_modulus + (2.0 * SHEAR_MODULUS / total_modulus) * ratio
            factor = jnp.where(load(flag_ref, 0, x, yb) > 0.5, soft, 1.0)
            mean = LAME_FIRST * vol
            s = [None] * 6
            for i in range(3):
                s[i] = (mean + factor * diag[i]) * quarter
                s[3 + i] = factor * off[i] * quarter
            if yb == nb - 1:
                s = [jnp.where(inside, v, 0.0) for v in s]
            stress.append([[s[0], s[3], s[4]], [s[3], s[1], s[5]], [s[4], s[5], s[2]]])
        new_carry = []
        for i in range(3):
            ax = [stress[yb][i][0] for yb in range(nb)]
            ay = [stress[yb][i][1] for yb in range(nb)]
            az = [stress[yb][i][2] for yb in range(nb)]
            ax_p = [roll_down(ax[-1])] + ax[:-1]
            ay_p = [roll_down(ay[-1])] + ay[:-1]
            az_p = [roll_down(az[-1])] + az[:-1]
            for yb in range(nb):
                fx = ax_p[yb] + ax[yb]
                fy = ay_p[yb] - ay[yb]
                fz = az_p[yb] + az[yb]
                back, front = fy - fx, fy + fx
                low, high = back - fz, back + fz
                if carry is not None:
                    low, high = low + carry[i * nb + yb][0], high + carry[i * nb + yb][1]
                if add_below is not None:
                    add_below(i, x, yb, low)
                if add_above is not None:
                    add_above(i, x, yb, high)
                new_carry.append((front - fz, front + fz))
        carry = new_carry
        here = there
    for i in range(3):
        for yb in range(nb):
            if add_below is not None:
                add_below(i, gx - 1, yb, carry[i * nb + yb][0])
            if add_above is not None:
                add_above(i, gx - 1, yb, carry[i * nb + yb][1])


def along_lanes(block, first, count):
    lane = lax.broadcasted_iota(jnp.int32, (LANES, LANES), 0)
    mask = jnp.where((lane >= first) & (lane < first + count), 1.0, 0.0).astype(BF16)
    return jnp.dot(block, mask, preferred_element_type=F32)


def scale_of(block):
    return along_lanes(block, 0, 3)


def flag_of(basis_ref, layer, n):
    start = 3 * n * layer
    return along_lanes(basis_ref[start : start + n, basis_ref.shape[1] - LANES :], 3, 1)


def times_transposed(a, b):
    return lax.dot_general(a, b, (((1,), (1,)), ((), ())), preferred_element_type=F32)


def rows_of(layer, rows):
    return pl.ds(pl.multiple_of(layer * rows, rows), rows)


def lift_layer(folded, coef, basis_ref, layer, disp_ref, send_ref, flag_row_ref):
    rows, rank = basis_ref.shape[0] // 2, basis_ref.shape[1] - LANES
    block = basis_ref[rows_of(layer, rows), :]
    if folded:
        lifted = times_transposed(block[:, :rank], coef)
    else:
        lifted = jnp.dot(block[:, :rank], coef, preferred_element_type=F32)
    disp = lifted * scale_of(block[:, rank:])
    disp_ref[...] = disp
    send_ref[:rows, :] = disp.astype(BF16)
    send_ref[rows:, :] = flag_row_ref[...].astype(BF16)


def far_kernel(folded, source_ref, basis_ref, flag_row_ref, disp_ref, send_ref, coef_ref):
    rank = basis_ref.shape[1] - LANES
    if folded:
        parts, _, half = source_ref.shape
        coef = source_ref[...].reshape(parts * SUB, half)
        per = SUB * half // rank
        for part in range(2):
            turn = unfold_matrix(parts, per, part).astype(BF16)
            coef_ref[:, part * half : (part + 1) * half] = jnp.dot(
                turn, coef, preferred_element_type=F32
            ).astype(BF16)
    else:
        coef = source_ref[...] if source_ref.ndim == 2 else source_ref[:, : source_ref.shape[1] - SUB, :]
        coef_ref[...] = coef.reshape(coef_ref.shape)
    odd = lax.rem(lax.axis_index("dom"), 2)
    lift_layer(folded, coef_ref[...], basis_ref, odd, disp_ref, send_ref, flag_row_ref)


def near_kernel(folded, coef_ref, basis_ref, flag_row_ref, disp_ref, send_ref):
    odd = lax.rem(lax.axis_index("dom"), 2)
    lift_layer(folded, coef_ref[...], basis_ref, 1 - odd, disp_ref, send_ref, flag_row_ref)


def putter(gx, n, f_ref, layer):
    def put(i, x, yb, value):
        start = (3 * layer + i) * n + (yb * gx + x) * SUB
        f_ref[start : start + SUB, :] = value

    return put


def own_kernel(gx, gy, rank, prepare, far_ref, near_ref, basis_ref, *refs):
    if prepare:
        start_ref, disp_ref, force_ref, coef_ref, scale_ref, flag_ref = refs
    else:
        disp_ref, force_ref, flag_ref = refs
    n, nb = gx * gy, gy // SUB
    flag_ref[...] = flag_of(basis_ref, 0, n)
    even = lax.rem(lax.axis_index("dom"), 2) == 0
    far, near = far_ref[...], near_ref[...]
    disp_ref[: 3 * n, :] = jnp.where(even, far, near)
    disp_ref[3 * n :, :] = jnp.where(even, near, far)
    put = functools.partial(putter, gx, n, force_ref)
    cell_forces(gx, nb, flag_ref, (disp_ref, 0), (disp_ref, 3 * n), put(0), put(1))
    if prepare:
        parts, depth, cases = start_ref.shape
        owned, per, spans = depth - SUB, cases // parts, LANES * parts // rank
        me = lax.axis_index("dom")
        rest = start_ref[:, owned:, :].astype(F32)
        rest = [jnp.sum(rest[k * spans : (k + 1) * spans], axis=0) for k in range(parts // spans)]
        rest = jnp.concatenate(rest, axis=1)
        pick = lax.broadcasted_iota(jnp.int32, (SUB, cases), 0)
        lane = lax.broadcasted_iota(jnp.int32, (SUB, cases), 1)
        pick = jnp.where((lane == pick + me * per) & (pick < per), 1.0, 0.0).astype(BF16)
        high = times_transposed(pick, start_ref[:, :owned, :].reshape(rank, cases))
        scale = jnp.sum(rest[per : per + 3, :], axis=0, keepdims=True)
        scale_ref[...] = fold(jnp.broadcast_to(scale, (SUB, rank)))
        coef_ref[...] = fold(high + rest)


def side_cells(gx, gy, remote_ref, is_next, disp_ref, flag, side_ref, side_flag_ref, force_ref):
    n, nb = gx * gy, gy // SUB
    layer = 3 * n
    remote = remote_ref[...].astype(F32)
    side_ref[:layer, :] = jnp.where(is_next, disp_ref[layer:, :], remote[:layer, :])
    side_ref[layer:, :] = jnp.where(is_next, remote[:layer, :], disp_ref[:layer, :])
    for row in range(n // LANES):
        theirs = column_of(remote[layer + row : layer + row + 1, :])
        where = slice(row * LANES, (row + 1) * LANES)
        side_flag_ref[where, :] = jnp.where(is_next, flag[where, :], jnp.broadcast_to(theirs, (LANES, LANES)))
    chosen = jnp.broadcast_to(is_next, (SUB, LANES))
    put = putter(gx, n, force_ref, 0)
    lows = {}

    def keep(i, x, yb, value):
        lows[i, x, yb] = value

    def choose(i, x, yb, value):
        put(i, x, yb, jnp.where(chosen, lows.pop((i, x, yb)), value))

    cell_forces(gx, nb, side_flag_ref, (side_ref, 0), (side_ref, layer), keep, choose)


def project(resid, basis_ref, layer, parts, scaled_ref):
    rows = resid.shape[0]
    rank = basis_ref.shape[1] - LANES
    block = basis_ref[rows_of(layer, rows), :]
    scaled_ref[...] = (resid * scale_of(block[:, rank:])).astype(BF16)
    if parts is None:
        return jnp.dot(scaled_ref[...].astype(F32).T.astype(BF16), block[:, :rank], preferred_element_type=F32)
    half, per = rank // 2, resid.shape[1] // parts
    total = None
    for part in range(2):
        turn = unfold_matrix(parts, per, part).T.astype(BF16)
        turned = times_transposed(turn, scaled_ref[...]).astype(BF16)
        term = jnp.dot(turned, block[:, part * half : (part + 1) * half], preferred_element_type=F32)
        total = term if total is None else total + term
    return total


def side_kernel(
    gx, gy, parts, remote_ref, disp_ref, force_ref, basis_ref, ext_hbm,
    resid_ref, rest_ref, total_ref, side_ref, side_flag_ref, near_force_ref, scaled_ref, ext_ref, sems,
):
    layer = 3 * gx * gy
    copies = start_copies((ext_hbm,), (ext_ref,), sems)
    odd = lax.rem(lax.axis_index("dom"), 2)
    flag = flag_of(basis_ref, 1, gx * gy)
    side_cells(gx, gy, remote_ref, odd == 0, disp_ref, flag, side_ref, side_flag_ref, near_force_ref)
    copies[0].wait()
    near_rows, far_rows = rows_of(1 - odd, layer), rows_of(odd, layer)
    rest_ref[...] = ext_ref[far_rows, :] - force_ref[far_rows, :]
    resid_ref[...] = ext_ref[near_rows, :] - force_ref[near_rows, :] - near_force_ref[...]
    total_ref[...] = project(resid_ref[...], basis_ref, 1 - odd, parts, scaled_ref)


def sweep_kernel(gx, gy, parts, remote_ref, disp_ref, rest_ref, total_ref, basis_ref, *refs):
    part_ref, *resid_refs, side_ref, side_flag_ref, far_force_ref, scaled_ref = refs
    me = lax.axis_index("dom")
    odd = lax.rem(me, 2)
    flag = flag_of(basis_ref, 1, gx * gy)
    side_cells(gx, gy, remote_ref, odd == 1, disp_ref, flag, side_ref, side_flag_ref, far_force_ref)
    resid = rest_ref[...] - jnp.where(me > 0, far_force_ref[...], 0.0)
    for ref in resid_refs:
        ref[...] = resid
    total = total_ref[...] + project(resid, basis_ref, odd, parts, scaled_ref)
    part_ref[...] = total.reshape(part_ref.shape).astype(part_ref.dtype)


def fold(value):
    half = value.shape[1] // 2
    row = lax.broadcasted_iota(jnp.int32, (SUB, half), 0)
    return jnp.where(row < SUB // 2, value[:, :half], pltpu.roll(value[:, half:], SUB // 2, 0))


def step(coef, update, rank):
    square = jnp.broadcast_to(jnp.sum(update * update, axis=1, keepdims=True), (SUB, LANES))
    square = (square + pltpu.roll(square, SUB // 2, 0))[:, 0:1]
    return coef + STEP_SIZE * update * lax.rsqrt(square / rank + EPSILON)


def middle_kernel(rank, parts_ref, start_ref, scale_ref, coef_ref, send_ref):
    update = scale_ref[...] * jnp.sum(parts_ref[...].astype(F32), axis=0)
    coef = step(start_ref[...], update, rank)
    coef_ref[...] = coef
    send_ref[...] = jnp.broadcast_to(coef.astype(BF16)[None], send_ref.shape)


def last_kernel(rank, owned, parts_ref, coef_ref, scale_ref, send_ref):
    update = scale_ref[...] * jnp.sum(parts_ref[...].astype(F32), axis=0)
    coef = step(coef_ref[...], update, rank)
    parts, spans = send_ref.shape[0], LANES // owned
    half = SUB // 2
    place = lax.broadcasted_iota(jnp.int32, (SUB, LANES), 1) // owned
    column = lax.rem(lax.broadcasted_iota(jnp.int32, (SUB, LANES), 0), half)
    for block in range(coef.shape[1] // LANES):
        value = coef[:, block * LANES : (block + 1) * LANES]
        turned = [value] + [pltpu.roll(value, shift * owned, 1) for shift in range(1, spans)]
        for span in range(spans):
            line = jnp.zeros_like(value)
            for shift in range(spans):
                line = jnp.where(lax.rem(column + spans - span, spans) == shift, turned[shift], line)
            line = jnp.where(place == column, line, 0.0)
            device = block * spans + span
            send_ref[device] = jnp.sum(line[:half], axis=0, keepdims=True)
            send_ref[parts // 2 + device] = jnp.sum(line[half:], axis=0, keepdims=True)


def finish_kernel(got_ref, out_ref):
    owned, cases = out_ref.shape
    parts = got_ref.shape[0]
    per = cases // parts
    got = jnp.concatenate([got_ref[source] for source in range(parts)], axis=0)
    got = jnp.concatenate([got] * (LANES // parts), axis=0).T
    source = lax.broadcasted_iota(jnp.int32, (LANES, cases), 0)
    case = lax.broadcasted_iota(jnp.int32, (LANES, cases), 1)
    total = None
    for column in range(per):
        high, rest = split2(got[column * owned : (column + 1) * owned, :])
        middle, low = split2(rest)
        turn = jnp.where((source < parts) & (case == source * per + column), 1.0, 0.0).astype(BF16)
        for value in (high, middle, low):
            term = jnp.dot(value.astype(BF16), turn, preferred_element_type=F32)
            total = term if total is None else total + term
    out_ref[...] = total


def unpermute_kernel(gx, gy, node_ref, near_ref, far_ref, out_ref, parts_ref):
    n = gx * gy
    rows, cases = out_ref.shape
    odd = lax.rem(lax.axis_index("dom"), 2)
    for ref, layer in ((near_ref, 1 - odd), (far_ref, odd)):
        high, low = split2(ref[...])
        parts_ref[rows_of(layer, 3 * n), :cases] = high.astype(BF16)
        parts_ref[rows_of(layer, 3 * n), cases:] = low.astype(BF16)
    node = node_ref[...]
    target = jnp.concatenate(
        [3.0 * node[:, layer * n : (layer + 1) * n] + i for layer in range(2) for i in range(3)], axis=1
    ).astype(jnp.int32)
    step = rows // 3
    for start in range(0, rows, step):
        here = lax.broadcasted_iota(jnp.int32, (step, rows), 0) + start
        pick = jnp.where(here == target, 1.0, 0.0).astype(BF16)
        both = jnp.dot(pick, parts_ref[...], preferred_element_type=F32)
        out_ref[start : start + step, :] = both[:, :cases] + both[:, cases:]


def call(kernel, outs, scratch=(), hbm=(), hbm_out=(), vmem=24, flops=0, nbytes=0):
    def run(*operands):
        shapes = [operands[i].shape for i in hbm]
        operands = [
            pltpu.with_memory_space_constraint(value, pltpu.HBM) if i in hbm else value
            for i, value in enumerate(operands)
        ]
        spaces = [pltpu.HBM if i in hbm else pltpu.VMEM for i in range(len(operands))]
        places = [
            pl.BlockSpec(memory_space=pltpu.HBM if i in hbm_out else pltpu.VMEM)
            for i in range(len(outs) if isinstance(outs, tuple) else 1)
        ]
        return pl.pallas_call(
            kernel,
            out_shape=outs,
            in_specs=[pl.BlockSpec(memory_space=space) for space in spaces],
            out_specs=tuple(places) if isinstance(outs, tuple) else places[0],
            scratch_shapes=[
                *scratch,
                *[pltpu.VMEM(shape, operands[i].dtype) for i, shape in zip(hbm, shapes)],
                *([pltpu.SemaphoreType.DMA((len(hbm),))] if hbm else []),
            ],
            compiler_params=pltpu.CompilerParams(vmem_limit_bytes=vmem << 20),
            cost_estimate=pl.CostEstimate(flops=flops, bytes_accessed=nbytes, transcendentals=0),
        )(*operands)

    return run


def on_device(coef_init, basis, basis_scale, ext_force, precond, connectivity, halo_nodes, plastic):
    parts = lax.axis_size("dom")
    rows, cases = ext_force.shape
    rank = basis.shape[1]
    owned = coef_init.shape[0]
    n = halo_nodes.shape[0]
    elems = connectivity.shape[0]
    gx, gy = grid_of(rows // 3, n, elems)
    tile = rows // basis_scale.shape[0]
    half = rank // 2
    layer = 3 * n
    folded = parts * (SUB // 2) == cases and LANES % owned == 0 and owned * (SUB // 2) == LANES
    shape = jax.ShapeDtypeStruct
    scratch = pltpu.VMEM

    def exchange(value):
        return lax.all_to_all(value, "dom", 0, 0)

    if folded:
        start = exchange(
            call(
                functools.partial(spread_kernel, parts), shape((parts, owned + SUB, cases), BF16), hbm=(0, 1)
            )(coef_init, precond.reshape(1, owned))
        )
    else:
        coef = lax.all_gather(coef_init, "dom", axis=0, tiled=True)
        scaling = lax.all_gather(precond, "dom", axis=0, tiled=True)
    basis_grid, ext_grid, flag_row, nodes = call(
        functools.partial(setup_kernel, gx, gy, tile),
        (
            shape((rows, rank + LANES), BF16),
            pltpu.HBM((rows, cases), F32),
            shape((SUB, LANES), F32),
            shape((1, 2 * n), F32),
        ),
        [scratch((rows, cases), F32), pltpu.SemaphoreType.DMA((1,))],
        hbm=(0, 1, 2, 3, 4, 5),
        hbm_out=(1,),
        flops=2 * rows * rows * (rank + 2 * cases),
        nbytes=4 * rows * rank,
    )(
        halo_nodes.reshape(1, n),
        basis_scale.reshape(1, -1),
        connectivity.T,
        plastic.reshape(1, elems),
        ext_force,
        basis,
    )
    near_pairs = [(d, d ^ 1) for d in range(parts)]
    far_pairs = [pair for d in range(1, parts - 1, 2) for pair in ((d, d + 1), (d + 1, d))]
    layer_disp, layer_sent = shape((layer, cases), F32), shape((layer + SUB, cases), BF16)
    side_scratch = [scratch((2 * layer, cases), F32), scratch((n, LANES), F32)]
    columns = shape((SUB, half), F32)
    for sweep in range(ITERS):
        second, last = folded and sweep > 0, sweep == ITERS - 1
        source = (send if second else start) if folded else coef.astype(BF16)
        far_disp, far, coef_rows = call(
            functools.partial(far_kernel, second),
            (layer_disp, layer_sent, shape((cases, rank) if second else (rank, cases), BF16)),
            flops=rows * rank * cases,
        )(source, basis_grid, flag_row)
        far = lax.ppermute(far, "dom", far_pairs)
        near_disp, near = call(
            functools.partial(near_kernel, second), (layer_disp, layer_sent), flops=rows * rank * cases
        )(coef_rows, basis_grid, flag_row)
        near = lax.ppermute(near, "dom", near_pairs)
        prepare = folded and sweep == 0
        disp, force, *mine = call(
            functools.partial(own_kernel, gx, gy, rank, prepare),
            (shape((rows, cases), F32), shape((rows, cases), F32), *([columns] * 2 if prepare else [])),
            [scratch((n, LANES), F32)],
            flops=rows * rank * cases,
        )(far_disp, near_disp, basis_grid, *([start] if prepare else []))
        if prepare:
            coef_mine, scale_mine = mine
        cut = parts if folded else None
        total_shape = (parts * SUB, half) if folded else (cases, rank)
        layer_scratch = [*side_scratch, scratch((layer, cases), F32), scratch((layer, cases), BF16)]
        resid_near, rest, total = call(
            functools.partial(side_kernel, gx, gy, cut),
            (layer_disp, layer_disp, shape(total_shape, F32)),
            layer_scratch,
            hbm=(4,),
            flops=rows * rank * cases,
        )(near, disp, force, basis_grid, ext_grid)
        part_shape = shape((parts, SUB, half), BF16) if folded else shape((cases, rank), F32)
        part, *resid_far = call(
            functools.partial(sweep_kernel, gx, gy, cut),
            (part_shape, *([layer_disp] if last else [])),
            layer_scratch,
            flops=2 * rows * rank * cases,
        )(far, disp, rest, total, basis_grid)
        if folded:
            part = exchange(part)
            if not last:
                coef_mine, send = call(
                    functools.partial(middle_kernel, rank), (columns, shape(part.shape, BF16))
                )(part, coef_mine, scale_mine)
                send = exchange(send)
        else:
            update = scaling[:, None] * lax.psum(part, "dom").T
            root = jnp.sqrt(jnp.sum(update * update, axis=0) / rank + EPSILON)
            coef = coef + STEP_SIZE * update / root
    nodal_residual = call(
        functools.partial(unpermute_kernel, gx, gy),
        shape((rows, cases), F32),
        [scratch((rows, 2 * cases), BF16)],
        flops=2 * rows * rows * 2 * cases,
    )(nodes, resid_near, resid_far[0])
    if folded:
        sent = call(functools.partial(last_kernel, rank, owned), shape((parts, 1, LANES), F32))(
            part, coef_mine, scale_mine
        )
        coef_out = call(finish_kernel, shape((owned, cases), F32))(exchange(sent))
    else:
        coef_out = lax.dynamic_slice_in_dim(coef, lax.axis_index("dom") * owned, owned, 0)
    return coef_out, nodal_residual


def solution(mesh):
    return jax.shard_map(
        on_device,
        mesh=mesh,
        in_specs=(
            P("dom", None),
            P("dom", None),
            P("dom"),
            P("dom", None),
            P("dom"),
            P("dom", None),
            P("dom"),
            P("dom"),
        ),
        out_specs=(P("dom", None), P("dom", None)),
        check_vma=False,
    )
```

```python
import functools
import math

import jax
import jax.numpy as jnp
from jax import lax
from jax.experimental import pallas as pl
from jax.experimental.pallas import tpu as pltpu
from jax.sharding import PartitionSpec as P

STEP_SIZE = 0.5
SHEAR_MODULUS = 1.0
LAME_FIRST = 1.5
HARDENING = 0.5
YIELD_STRESS = 3.0
EPSILON = 1e-05
ITERS = 2
LANES = 128
SUB = 8
F32 = jnp.float32
BF16 = jnp.bfloat16


def grid_of(node_count, halo_count, elem_count):
    layers = node_count // halo_count
    assert layers == 2
    total = halo_count + 1 - elem_count // layers
    root = math.isqrt(total * total - 4 * halo_count)
    gx = (total + root) // 2
    gy = halo_count // gx
    assert gx * gy == halo_count and (gx - 1) * (gy - 1) * layers == elem_count
    assert gx == gy and gy % SUB == 0
    return gx, gy


def grid_index(p, gx, gy):
    nb = gy // SUB
    q, s = p // SUB, p % SUB
    return (nb * s + q // gx) * gx + q % gx


def column_of(row):
    n = row.shape[1]
    eye = lax.broadcasted_iota(jnp.int32, (n, n), 0) == lax.broadcasted_iota(jnp.int32, (n, n), 1)
    return jnp.sum(jnp.where(eye, row, 0.0), axis=1, keepdims=True)


def row_of(col):
    n = col.shape[0]
    eye = lax.broadcasted_iota(jnp.int32, (n, n), 0) == lax.broadcasted_iota(jnp.int32, (n, n), 1)
    return jnp.sum(jnp.where(eye, col, 0.0), axis=0, keepdims=True)


def split2(value):
    high = value.astype(BF16).astype(F32)
    return high, value - high


def first_layer_column(halo_row, gx, gy):
    n = gx * gy
    want = grid_index(lax.broadcasted_iota(jnp.int32, (n, n), 0), gx, gy)
    hit = lax.broadcasted_iota(jnp.int32, (n, n), 1) == want
    return jnp.sum(jnp.where(hit, halo_row, 0.0), axis=1, keepdims=True)


def select_rows(node_col, i, rows):
    n = node_col.shape[0]
    pick = (3.0 * node_col + i).astype(jnp.int32)
    return jnp.where(lax.broadcasted_iota(jnp.int32, (n, rows), 1) == pick, 1.0, 0.0).astype(BF16)


def scale_block(node_row, i, scale_col, tile, flag_row):
    tiles, n = scale_col.shape[0], node_row.shape[1]
    row = 3.0 * node_row + i
    low = lax.broadcasted_iota(jnp.int32, (tiles, n), 0).astype(F32) * tile
    scale = jnp.sum(jnp.where((row >= low) & (row < low + tile), scale_col, 0.0), axis=0, keepdims=True)
    high, rest = split2(scale)
    middle, last = split2(rest)
    place = lax.broadcasted_iota(jnp.int32, (SUB, n), 0)
    block = jnp.zeros((SUB, n), F32)
    for index, value in enumerate((high, middle, last, flag_row)):
        block = jnp.where(place == index, value, block)
    return block.astype(BF16)


def start_copies(sources, targets, sems):
    copies = [pltpu.make_async_copy(a, b, sems.at[i]) for i, (a, b) in enumerate(zip(sources, targets))]
    for copy in copies:
        copy.start()
    return copies


def spread_kernel(parts, coef_hbm, precond_hbm, out_hbm, high_ref, rest_ref, out_sems, coef_ref, precond_ref, sems):
    owned, cases = coef_ref.shape
    per, spans = cases // parts, LANES // owned
    for copy in start_copies((coef_hbm, precond_hbm), (coef_ref, precond_ref), sems):
        copy.wait()
    high, low = split2(coef_ref[...])
    high_ref[...] = jnp.broadcast_to(high.astype(BF16)[None], (parts, owned, cases))
    (high_copy,) = start_copies((high_ref,), (out_hbm.at[:, :owned, :],), out_sems)
    mine = lax.rem(lax.axis_index("dom"), spans)
    lane = lax.broadcasted_iota(jnp.int32, (1, LANES), 1) // owned
    low = jnp.concatenate([low] * spans, axis=0).T
    low = jnp.where(lane == mine, low, 0.0).astype(BF16)
    rest = jnp.dot(fold_matrix(parts, per, 0), low, preferred_element_type=F32)
    scale = jnp.where(lane == mine, jnp.concatenate([precond_ref[...]] * spans, axis=1), 0.0)
    first, scale = split2(scale)
    second, third = split2(scale)
    row = lax.rem(lax.broadcasted_iota(jnp.int32, (parts * SUB, LANES), 0), SUB) - per
    rest = rest + jnp.where(row == 0, first, jnp.where(row == 1, second, jnp.where(row == 2, third, 0.0)))
    rest_ref[...] = rest.reshape(parts, SUB, LANES).astype(BF16)
    rest_copy = pltpu.make_async_copy(rest_ref, out_hbm.at[:, owned:, :], out_sems.at[1])
    rest_copy.start()
    high_copy.wait()
    rest_copy.wait()


def unfold_matrix(parts, per, half):
    cases = parts * per
    c = lax.broadcasted_iota(jnp.int32, (cases, parts * SUB), 0)
    row = lax.broadcasted_iota(jnp.int32, (cases, parts * SUB), 1)
    return jnp.where(row == (c // per) * SUB + lax.rem(c, per) + half * per, 1.0, 0.0)


def fold_matrix(parts, per, half):
    row = lax.broadcasted_iota(jnp.int32, (parts * SUB, parts * per), 0)
    case = lax.broadcasted_iota(jnp.int32, (parts * SUB, parts * per), 1)
    place = row % SUB - half * per
    here = (place >= 0) & (place < per) & (case == row // SUB * per + place)
    return jnp.where(here, 1.0, 0.0).astype(BF16)


def setup_kernel(
    gx, gy, tile, halo_hbm, scale_hbm, conn_hbm, plastic_hbm, ext_hbm, basis_hbm,
    out_ref, scale_out_ref, ext_out, flag_row_ref, node_ref,
    ext_grid_ref, out_sems, halo_ref, scale_ref, conn_ref, plastic_ref, ext_ref, basis_ref, sems,
):
    n = gx * gy
    rows, _ = basis_ref.shape
    copies = start_copies(
        (halo_hbm, scale_hbm, conn_hbm, plastic_hbm, ext_hbm, basis_hbm),
        (halo_ref, scale_ref, conn_ref, plastic_ref, ext_ref, basis_ref),
        sems,
    )
    for copy in copies[:4]:
        copy.wait()
    conn = conn_ref[...].astype(F32)
    elems = conn.shape[1]
    place = grid_index(lax.broadcasted_iota(jnp.int32, (n, elems), 0), gx, gy).astype(F32) + 2 * n
    node0 = first_layer_column(halo_ref[...].astype(F32), gx, gy)
    node1 = jnp.full((n, 1), -1.0, F32)
    for corner in range(4):
        hit = conn[4 + corner : 5 + corner, :] == place
        found = jnp.max(jnp.where(hit, conn[corner : corner + 1, :], -1.0), axis=1, keepdims=True)
        node1 = jnp.maximum(node1, found)
    active = (plastic_ref[...] == 1).astype(F32)
    cells = (conn[0:1, :] == jnp.broadcast_to(node0, (n, elems)), conn[4:5, :] == place)
    flags = [jnp.max(jnp.where(hit, active, 0.0), axis=1, keepdims=True) for hit in cells]
    flag_row_ref[...] = jnp.zeros_like(flag_row_ref)
    flag_rows = [row_of(flag) for flag in flags]
    flag = flag_rows[1]
    scale_col = column_of(scale_ref[...])
    node_rows = [row_of(node0), row_of(node1)]
    for row in range(n // LANES):
        flag_row_ref[row : row + 1, :] = flag[:, row * LANES : (row + 1) * LANES]
    node_ref[...] = jnp.concatenate(node_rows, axis=1)
    copies[4].wait()
    high, low = split2(ext_ref[...])
    cases = ext_ref.shape[1]
    loads = jnp.concatenate([high.astype(BF16), low.astype(BF16)], axis=1)
    copies[5].wait()
    out_copies = []
    for layer, node in enumerate((node0, node1)):
        for i in range(3):
            start = (3 * layer + i) * n
            pick = select_rows(node, i, rows)
            both = jnp.dot(pick, loads, preferred_element_type=F32)
            ext_grid_ref[start : start + n, :] = both[:, :cases] + both[:, cases:]
            if i == 2:
                done = slice(3 * n * layer, 3 * n * (layer + 1))
                out_copies.append(
                    pltpu.make_async_copy(ext_grid_ref.at[done, :], ext_out.at[done, :], out_sems.at[layer])
                )
                out_copies[-1].start()
            scale_out_ref[layer, :, i * n : (i + 1) * n] = scale_block(
                node_rows[layer], i, scale_col, tile, flag_rows[layer]
            )
            out_ref[start : start + n, :] = jnp.dot(
                pick, basis_ref[...], preferred_element_type=F32
            ).astype(BF16)
    for copy in out_copies:
        copy.wait()


def cell_forces(gx, nb, flag_ref, below, above, add_below, add_above):
    quarter = 0.25
    n = gx * nb * SUB

    def load(ref, first, x, yb):
        start = first + (yb * gx + x) * SUB
        return ref[start : start + SUB, :]

    def level(x):
        total, jump = [], []
        for i in range(3):
            low = [load(below[0], below[1] + i * n, x, yb) for yb in range(nb)]
            high = [load(above[0], above[1] + i * n, x, yb) for yb in range(nb)]
            total.append([a + b for a, b in zip(low, high)])
            jump.append([b - a for a, b in zip(low, high)])
        return total, jump

    def roll_up(v):
        return pltpu.roll(v, SUB - 1, 0)

    def roll_down(v):
        return pltpu.roll(v, 1, 0)

    inside = lax.broadcasted_iota(jnp.int32, (SUB, LANES), 0) < SUB - 1
    total_modulus = 2.0 * SHEAR_MODULUS + HARDENING
    here = level(0)
    carry = None
    for x in range(gx - 1):
        there = level(x + 1)
        grad = [[[None] * 3 for _ in range(3)] for _ in range(nb)]
        for i in range(3):
            sum_x = [a + b for a, b in zip(here[0][i], there[0][i])]
            dif_x = [b - a for a, b in zip(here[0][i], there[0][i])]
            jmp_x = [a + b for a, b in zip(here[1][i], there[1][i])]
            sum_n = sum_x[1:] + [roll_up(sum_x[0])]
            dif_n = dif_x[1:] + [roll_up(dif_x[0])]
            jmp_n = jmp_x[1:] + [roll_up(jmp_x[0])]
            for yb in range(nb):
                grad[yb][i][0] = dif_x[yb] + dif_n[yb]
                grad[yb][i][1] = sum_n[yb] - sum_x[yb]
                grad[yb][i][2] = jmp_x[yb] + jmp_n[yb]
        stress = []
        for yb in range(nb):
            g = grad[yb]
            vol = (g[0][0] + g[1][1] + g[2][2]) * quarter
            third = vol * (2.0 * SHEAR_MODULUS / 3.0)
            diag = [g[i][i] * (2.0 * SHEAR_MODULUS * quarter) - third for i in range(3)]
            off = [
                (g[i][j] + g[j][i]) * (SHEAR_MODULUS * quarter) for i, j in ((0, 1), (0, 2), (1, 2))
            ]
            norm = diag[0] * diag[0] + diag[1] * diag[1] + diag[2] * diag[2]
            norm = norm + 2.0 * (off[0] * off[0] + off[1] * off[1] + off[2] * off[2])
            ratio = YIELD_STRESS * lax.rsqrt(jnp.maximum(norm, YIELD_STRESS * YIELD_STRESS))
            soft = HARDENING / total_modulus + (2.0 * SHEAR_MODULUS / total_modulus) * ratio
            factor = jnp.where(load(flag_ref, 0, x, yb) > 0.5, soft, 1.0)
            mean = LAME_FIRST * vol
            s = [None] * 6
            for i in range(3):
                s[i] = (mean + factor * diag[i]) * quarter
                s[3 + i] = factor * off[i] * quarter
            if yb == nb - 1:
                s = [jnp.where(inside, v, 0.0) for v in s]
            stress.append([[s[0], s[3], s[4]], [s[3], s[1], s[5]], [s[4], s[5], s[2]]])
        new_carry = []
        for i in range(3):
            ax = [stress[yb][i][0] for yb in range(nb)]
            ay = [stress[yb][i][1] for yb in range(nb)]
            az = [stress[yb][i][2] for yb in range(nb)]
            ax_p = [roll_down(ax[-1])] + ax[:-1]
            ay_p = [roll_down(ay[-1])] + ay[:-1]
            az_p = [roll_down(az[-1])] + az[:-1]
            for yb in range(nb):
                fx = ax_p[yb] + ax[yb]
                fy = ay_p[yb] - ay[yb]
                fz = az_p[yb] + az[yb]
                back, front = fy - fx, fy + fx
                low, high = back - fz, back + fz
                if carry is not None:
                    low, high = low + carry[i * nb + yb][0], high + carry[i * nb + yb][1]
                if add_below is not None:
                    add_below(i, x, yb, low)
                if add_above is not None:
                    add_above(i, x, yb, high)
                new_carry.append((front - fz, front + fz))
        carry = new_carry
        here = there
    for i in range(3):
        for yb in range(nb):
            if add_below is not None:
                add_below(i, gx - 1, yb, carry[i * nb + yb][0])
            if add_above is not None:
                add_above(i, gx - 1, yb, carry[i * nb + yb][1])


def along_lanes(block, first, count):
    row = lax.broadcasted_iota(jnp.int32, (SUB, LANES), 0)
    mask = jnp.where((row >= first) & (row < first + count), 1.0, 0.0).astype(BF16)
    return lax.dot_general(block, mask, (((0,), (0,)), ((), ())), preferred_element_type=F32)


def scale_of(scale_ref, layer):
    return along_lanes(scale_ref[layer], 0, 3)


def flag_of(scale_ref, layer, n):
    return along_lanes(scale_ref[layer, :, :n], 3, 1)


def times_transposed(a, b):
    return lax.dot_general(a, b, (((1,), (1,)), ((), ())), preferred_element_type=F32)


def rows_of(layer, rows):
    return pl.ds(pl.multiple_of(layer * rows, rows), rows)


def lift_layer(folded, coef, basis_ref, scale_ref, layer, disp_ref, send_ref, flag_row_ref):
    rows = basis_ref.shape[0] // 2
    block = basis_ref[rows_of(layer, rows), :]
    if folded:
        lifted = times_transposed(block, coef)
    else:
        lifted = jnp.dot(block, coef, preferred_element_type=F32)
    disp = lifted * scale_of(scale_ref, layer)
    disp_ref[...] = disp
    send_ref[:rows, :] = disp.astype(BF16)
    send_ref[rows:, :] = flag_row_ref[...].astype(BF16)


def far_kernel(same_ref, other_ref, basis_ref, scale_ref, flag_row_ref, disp_ref, send_ref, coef_ref, source_ref):
    rank = basis_ref.shape[1]
    chips, _, half = same_ref.shape
    core = lax.rem(lax.axis_index("dom"), 2)
    source_ref[:, core] = same_ref[...]
    source_ref[:, 1 - core] = other_ref[...]
    coef = source_ref[...].reshape(chips * 2 * SUB, half)
    per = SUB * half // rank
    for part in range(2):
        turn = unfold_matrix(2 * chips, per, part).astype(BF16)
        coef_ref[:, part * half : (part + 1) * half] = jnp.dot(
            turn, coef, preferred_element_type=F32
        ).astype(BF16)
    lift_layer(True, coef_ref[...], basis_ref, scale_ref, core, disp_ref, send_ref, flag_row_ref)


def first_far_kernel(owned, source_ref, basis_ref, scale_ref, flag_row_ref, disp_ref, send_ref, coef_ref):
    coef_ref[...] = source_ref[:, :owned, :].reshape(coef_ref.shape)
    odd = lax.rem(lax.axis_index("dom"), 2)
    lift_layer(False, coef_ref[...], basis_ref, scale_ref, odd, disp_ref, send_ref, flag_row_ref)


def near_kernel(folded, coef_ref, basis_ref, scale_ref, flag_row_ref, disp_ref, send_ref):
    odd = lax.rem(lax.axis_index("dom"), 2)
    lift_layer(folded, coef_ref[...], basis_ref, scale_ref, 1 - odd, disp_ref, send_ref, flag_row_ref)


def putter(gx, n, f_ref, layer):
    def put(i, x, yb, value):
        start = (3 * layer + i) * n + (yb * gx + x) * SUB
        f_ref[start : start + SUB, :] = value

    return put


def own_kernel(gx, gy, rank, prepare, far_ref, near_ref, scale_in_ref, *refs):
    if prepare:
        start_ref, disp_ref, force_ref, coef_ref, scale_ref, flag_ref = refs
    else:
        disp_ref, force_ref, flag_ref = refs
    n, nb = gx * gy, gy // SUB
    flag_ref[...] = flag_of(scale_in_ref, 0, n)
    even = lax.rem(lax.axis_index("dom"), 2) == 0
    far, near = far_ref[...], near_ref[...]
    disp_ref[: 3 * n, :] = jnp.where(even, far, near)
    disp_ref[3 * n :, :] = jnp.where(even, near, far)
    put = functools.partial(putter, gx, n, force_ref)
    cell_forces(gx, nb, flag_ref, (disp_ref, 0), (disp_ref, 3 * n), put(0), put(1))
    if prepare:
        parts, depth, cases = start_ref.shape
        owned, per, spans = depth - SUB, cases // parts, LANES * parts // rank
        me = lax.axis_index("dom")
        rest = start_ref[:, owned:, :].astype(F32)
        rest = [jnp.sum(rest[k * spans : (k + 1) * spans], axis=0) for k in range(parts // spans)]
        rest = jnp.concatenate(rest, axis=1)
        pick = lax.broadcasted_iota(jnp.int32, (SUB, cases), 0)
        lane = lax.broadcasted_iota(jnp.int32, (SUB, cases), 1)
        pick = jnp.where((lane == pick + me * per) & (pick < per), 1.0, 0.0).astype(BF16)
        high = times_transposed(pick, start_ref[:, :owned, :].reshape(rank, cases))
        scale = jnp.sum(rest[per : per + 3, :], axis=0, keepdims=True)
        scale_ref[...] = fold(jnp.broadcast_to(scale, (SUB, rank)))
        coef_ref[...] = fold(high + rest)


def side_cells(gx, gy, remote_ref, is_next, disp_ref, flag, side_ref, side_flag_ref, force_ref):
    n, nb = gx * gy, gy // SUB
    layer = 3 * n
    remote = remote_ref[...].astype(F32)
    side_ref[:layer, :] = jnp.where(is_next, disp_ref[layer:, :], remote[:layer, :])
    side_ref[layer:, :] = jnp.where(is_next, remote[:layer, :], disp_ref[:layer, :])
    for row in range(n // LANES):
        theirs = column_of(remote[layer + row : layer + row + 1, :])
        where = slice(row * LANES, (row + 1) * LANES)
        side_flag_ref[where, :] = jnp.where(is_next, flag[where, :], jnp.broadcast_to(theirs, (LANES, LANES)))
    chosen = jnp.broadcast_to(is_next, (SUB, LANES))
    put = putter(gx, n, force_ref, 0)
    lows = {}

    def keep(i, x, yb, value):
        lows[i, x, yb] = value

    def choose(i, x, yb, value):
        put(i, x, yb, jnp.where(chosen, lows.pop((i, x, yb)), value))

    cell_forces(gx, nb, side_flag_ref, (side_ref, 0), (side_ref, layer), keep, choose)


def project(resid, basis_ref, scale_ref, layer, parts, scaled_ref):
    rows = resid.shape[0]
    rank = basis_ref.shape[1]
    block = basis_ref[rows_of(layer, rows), :]
    scaled_ref[...] = (resid * scale_of(scale_ref, layer)).astype(BF16)
    if parts is None:
        return jnp.dot(scaled_ref[...].astype(F32).T.astype(BF16), block, preferred_element_type=F32)
    half, per = rank // 2, resid.shape[1] // parts
    total = None
    for part in range(2):
        turn = fold_matrix(parts, per, part)
        turned = times_transposed(turn, scaled_ref[...]).astype(BF16)
        term = jnp.dot(turned, block[:, part * half : (part + 1) * half], preferred_element_type=F32)
        total = term if total is None else total + term
    return total


def side_kernel(
    gx, gy, parts, remote_ref, disp_ref, force_ref, basis_ref, scale_ref, ext_hbm,
    resid_hbm, rest_ref, total_ref, side_ref, side_flag_ref, near_force_ref, scaled_ref, resid_ref, out_sems, ext_ref, sems,
):
    layer = 3 * gx * gy
    copies = start_copies((ext_hbm,), (ext_ref,), sems)
    odd = lax.rem(lax.axis_index("dom"), 2)
    flag = flag_of(scale_ref, 1, gx * gy)
    side_cells(gx, gy, remote_ref, odd == 0, disp_ref, flag, side_ref, side_flag_ref, near_force_ref)
    copies[0].wait()
    near_rows, far_rows = rows_of(1 - odd, layer), rows_of(odd, layer)
    rest_ref[...] = ext_ref[far_rows, :] - force_ref[far_rows, :]
    resid_ref[...] = ext_ref[near_rows, :] - force_ref[near_rows, :] - near_force_ref[...]
    out_copies = start_copies((resid_ref,), (resid_hbm,), out_sems)
    total_ref[...] = project(resid_ref[...], basis_ref, scale_ref, 1 - odd, parts, scaled_ref)
    out_copies[0].wait()


def sweep_kernel(gx, gy, parts, remote_ref, disp_ref, rest_ref, total_ref, basis_ref, scale_ref, *refs):
    part_ref, *resid_hbm, side_ref, side_flag_ref, far_force_ref, scaled_ref, resid_ref, out_sems = refs
    me = lax.axis_index("dom")
    odd = lax.rem(me, 2)
    flag = flag_of(scale_ref, 1, gx * gy)
    side_cells(gx, gy, remote_ref, odd == 1, disp_ref, flag, side_ref, side_flag_ref, far_force_ref)
    resid = rest_ref[...] - jnp.where(me > 0, far_force_ref[...], 0.0)
    resid_ref[...] = resid
    out_copies = start_copies([resid_ref] * len(resid_hbm), resid_hbm, out_sems)
    total = total_ref[...] + project(resid, basis_ref, scale_ref, odd, parts, scaled_ref)
    part_ref[...] = total.reshape(part_ref.shape).astype(part_ref.dtype)
    for copy in out_copies:
        copy.wait()


def fold(value):
    half = value.shape[1] // 2
    row = lax.broadcasted_iota(jnp.int32, (SUB, half), 0)
    return jnp.where(row < SUB // 2, value[:, :half], pltpu.roll(value[:, half:], SUB // 2, 0))


def step(coef, update, rank):
    square = jnp.broadcast_to(jnp.sum(update * update, axis=1, keepdims=True), (SUB, LANES))
    square = (square + pltpu.roll(square, SUB // 2, 0))[:, 0:1]
    return coef + STEP_SIZE * update * lax.rsqrt(square / rank + EPSILON)


def middle_kernel(rank, parts_ref, start_ref, scale_ref, coef_ref, send_ref):
    update = scale_ref[...] * jnp.sum(parts_ref[...].astype(F32), axis=0)
    coef = step(start_ref[...], update, rank)
    coef_ref[...] = coef
    send_ref[...] = jnp.broadcast_to(coef.astype(BF16)[None], send_ref.shape)


def last_kernel(rank, owned, parts_ref, coef_ref, scale_ref, send_ref):
    update = scale_ref[...] * jnp.sum(parts_ref[...].astype(F32), axis=0)
    coef = step(coef_ref[...], update, rank)
    parts, spans = send_ref.shape[0], LANES // owned
    half = SUB // 2
    place = lax.broadcasted_iota(jnp.int32, (SUB, LANES), 1) // owned
    column = lax.rem(lax.broadcasted_iota(jnp.int32, (SUB, LANES), 0), half)
    for block in range(coef.shape[1] // LANES):
        value = coef[:, block * LANES : (block + 1) * LANES]
        turned = [value] + [pltpu.roll(value, shift * owned, 1) for shift in range(1, spans)]
        for span in range(spans):
            line = jnp.zeros_like(value)
            for shift in range(spans):
                line = jnp.where(lax.rem(column + spans - span, spans) == shift, turned[shift], line)
            line = jnp.where(place == column, line, 0.0)
            device = block * spans + span
            send_ref[device] = jnp.sum(line[:half], axis=0, keepdims=True)
            send_ref[parts // 2 + device] = jnp.sum(line[half:], axis=0, keepdims=True)


def finish_kernel(got_ref, out_ref):
    owned, cases = out_ref.shape
    parts = got_ref.shape[0]
    per = cases // parts
    got = jnp.concatenate([got_ref[source] for source in range(parts)], axis=0)
    got = jnp.concatenate([got] * per, axis=0).T
    place = lax.broadcasted_iota(jnp.int32, (owned, LANES), 1) // parts
    line = jnp.zeros((owned, LANES), F32)
    for column in range(per):
        line = jnp.where(place == column, got[column * owned : (column + 1) * owned, :], line)
    place = lax.broadcasted_iota(jnp.int32, (LANES, cases), 0)
    case = lax.broadcasted_iota(jnp.int32, (LANES, cases), 1)
    turn = jnp.where(case == lax.rem(place, parts) * per + place // parts, 1.0, 0.0).astype(BF16)
    high, rest = split2(line)
    middle, low = split2(rest)
    value = jnp.concatenate([high.astype(BF16), middle.astype(BF16), low.astype(BF16)], axis=0)
    turned = jnp.dot(value, turn, preferred_element_type=F32)
    out_ref[...] = turned[:owned] + turned[owned : 2 * owned] + turned[2 * owned :]


def unpermute_kernel(gx, gy, node_ref, near_hbm, far_hbm, out_ref, parts_ref, near_ref, far_ref, sems):
    n = gx * gy
    rows, cases = out_ref.shape
    copies = start_copies((near_hbm, far_hbm), (near_ref, far_ref), sems)
    node = node_ref[...]
    target = jnp.concatenate(
        [3.0 * node[:, layer * n : (layer + 1) * n] + i for layer in range(2) for i in range(3)], axis=1
    ).astype(jnp.int32)
    step = rows // 3
    picks = [
        jnp.where(lax.broadcasted_iota(jnp.int32, (step, rows), 0) + start == target, 1.0, 0.0).astype(BF16)
        for start in range(0, rows, step)
    ]
    odd = lax.rem(lax.axis_index("dom"), 2)
    for copy, ref, layer in zip(copies, (near_ref, far_ref), (1 - odd, odd)):
        copy.wait()
        high, low = split2(ref[...])
        parts_ref[rows_of(layer, 3 * n), :cases] = high.astype(BF16)
        parts_ref[rows_of(layer, 3 * n), cases:] = low.astype(BF16)
    for i, pick in enumerate(picks):
        both = jnp.dot(pick, parts_ref[...], preferred_element_type=F32)
        out_ref[i * step : (i + 1) * step, :] = both[:, :cases] + both[:, cases:]


def call(kernel, outs, scratch=(), hbm=(), hbm_out=(), vmem=24, flops=0, nbytes=0):
    def run(*operands):
        shapes = [operands[i].shape for i in hbm]
        operands = [
            pltpu.with_memory_space_constraint(value, pltpu.HBM) if i in hbm else value
            for i, value in enumerate(operands)
        ]
        spaces = [pltpu.HBM if i in hbm else pltpu.VMEM for i in range(len(operands))]
        places = [
            pl.BlockSpec(memory_space=pltpu.HBM if i in hbm_out else pltpu.VMEM)
            for i in range(len(outs) if isinstance(outs, tuple) else 1)
        ]
        return pl.pallas_call(
            kernel,
            out_shape=outs,
            in_specs=[pl.BlockSpec(memory_space=space) for space in spaces],
            out_specs=tuple(places) if isinstance(outs, tuple) else places[0],
            scratch_shapes=[
                *scratch,
                *[pltpu.VMEM(shape, operands[i].dtype) for i, shape in zip(hbm, shapes)],
                *([pltpu.SemaphoreType.DMA((len(hbm),))] if hbm else []),
            ],
            compiler_params=pltpu.CompilerParams(vmem_limit_bytes=vmem << 20),
            cost_estimate=pl.CostEstimate(flops=flops, bytes_accessed=nbytes, transcendentals=0),
        )(*operands)

    return run


def on_device(coef_init, basis, basis_scale, ext_force, precond, connectivity, halo_nodes, plastic):
    parts = lax.axis_size("dom")
    rows, cases = ext_force.shape
    rank = basis.shape[1]
    owned = coef_init.shape[0]
    n = halo_nodes.shape[0]
    elems = connectivity.shape[0]
    gx, gy = grid_of(rows // 3, n, elems)
    tile = rows // basis_scale.shape[0]
    half = rank // 2
    layer = 3 * n
    folded = parts * (SUB // 2) == cases and LANES % owned == 0 and owned * (SUB // 2) == LANES
    shape = jax.ShapeDtypeStruct
    scratch = pltpu.VMEM

    chips = parts // 2
    near_pairs = [(d, d ^ 1) for d in range(parts)]

    def exchange(value):
        return lax.all_to_all(value, "dom", 0, 0)

    def exchange_chips(value):
        groups = [list(range(core, parts, 2)) for core in range(2)]
        return lax.all_to_all(value, "dom", 0, 0, axis_index_groups=groups)

    if folded:
        start = exchange(
            call(
                functools.partial(spread_kernel, parts),
                pltpu.HBM((parts, owned + SUB, cases), BF16),
                [
                    scratch((parts, owned, cases), BF16),
                    scratch((parts, SUB, cases), BF16),
                    pltpu.SemaphoreType.DMA((2,)),
                ],
                hbm=(0, 1),
                hbm_out=(0,),
            )(coef_init, precond.reshape(1, owned))
        )
    else:
        coef = lax.all_gather(coef_init, "dom", axis=0, tiled=True)
        scaling = lax.all_gather(precond, "dom", axis=0, tiled=True)
    basis_grid, scale_grid, ext_grid, flag_row, nodes = call(
        functools.partial(setup_kernel, gx, gy, tile),
        (
            shape((rows, rank), BF16),
            shape((2, SUB, layer), BF16),
            pltpu.HBM((rows, cases), F32),
            shape((SUB, LANES), F32),
            shape((1, 2 * n), F32),
        ),
        [scratch((rows, cases), F32), pltpu.SemaphoreType.DMA((2,))],
        hbm=(0, 1, 2, 3, 4, 5),
        hbm_out=(2,),
        flops=2 * rows * rows * (rank + 2 * cases),
        nbytes=4 * rows * rank,
    )(
        halo_nodes.reshape(1, n),
        basis_scale.reshape(1, -1),
        connectivity.T,
        plastic.reshape(1, elems),
        ext_force,
        basis,
    )
    far_pairs = [pair for d in range(1, parts - 1, 2) for pair in ((d, d + 1), (d + 1, d))]
    layer_disp, layer_sent = shape((layer, cases), F32), shape((layer + SUB, cases), BF16)
    side_scratch = [scratch((2 * layer, cases), F32), scratch((n, LANES), F32)]
    columns = shape((SUB, half), F32)
    for sweep in range(ITERS):
        second, last = folded and sweep > 0, sweep == ITERS - 1
        first_source = start if folded else coef.astype(BF16).reshape(parts, owned, cases)
        source = send if second else (first_source,)
        far_disp, far, coef_rows = call(
            far_kernel if second else functools.partial(first_far_kernel, owned),
            (layer_disp, layer_sent, shape((cases, rank) if second else (rank, cases), BF16)),
            [scratch((chips, 2, SUB, half), BF16)] if second else (),
            flops=rows * rank * cases,
        )(*source, basis_grid, scale_grid, flag_row)
        far = lax.ppermute(far, "dom", far_pairs)
        near_disp, near = call(
            functools.partial(near_kernel, second), (layer_disp, layer_sent), flops=rows * rank * cases
        )(coef_rows, basis_grid, scale_grid, flag_row)
        near = lax.ppermute(near, "dom", near_pairs)
        prepare = folded and sweep == 0
        disp, force, *mine = call(
            functools.partial(own_kernel, gx, gy, rank, prepare),
            (shape((rows, cases), F32), shape((rows, cases), F32), *([columns] * 2 if prepare else [])),
            [scratch((n, LANES), F32)],
            flops=rows * rank * cases,
        )(far_disp, near_disp, scale_grid, *([start] if prepare else []))
        if prepare:
            coef_mine, scale_mine = mine
        cut = parts if folded else None
        total_shape = (parts * SUB, half) if folded else (cases, rank)
        layer_scratch = [
            *side_scratch,
            scratch((layer, cases), F32),
            scratch((layer, cases), BF16),
            scratch((layer, cases), F32),
            pltpu.SemaphoreType.DMA((1,)),
        ]
        resid_near, rest, total = call(
            functools.partial(side_kernel, gx, gy, cut),
            (pltpu.HBM((layer, cases), F32), layer_disp, shape(total_shape, F32)),
            layer_scratch,
            hbm=(5,),
            hbm_out=(0,),
            flops=rows * rank * cases,
        )(near, disp, force, basis_grid, scale_grid, ext_grid)
        part_shape = shape((parts, SUB, half), BF16) if folded else shape((cases, rank), F32)
        part, *resid_far = call(
            functools.partial(sweep_kernel, gx, gy, cut),
            (part_shape, *([pltpu.HBM((layer, cases), F32)] if last else [])),
            layer_scratch,
            hbm_out=(1,) if last else (),
            flops=2 * rows * rank * cases,
        )(far, disp, rest, total, basis_grid, scale_grid)
        if folded:
            part = exchange(part)
            if not last:
                coef_mine, send = call(
                    functools.partial(middle_kernel, rank), (columns, shape((chips, SUB, half), BF16))
                )(part, coef_mine, scale_mine)
                send = exchange_chips(send)
                send = send, lax.ppermute(send, "dom", near_pairs)
        else:
            update = scaling[:, None] * lax.psum(part, "dom").T
            root = jnp.sqrt(jnp.sum(update * update, axis=0) / rank + EPSILON)
            coef = coef + STEP_SIZE * update / root
    nodal_residual = call(
        functools.partial(unpermute_kernel, gx, gy),
        shape((rows, cases), F32),
        [scratch((rows, 2 * cases), BF16)],
        hbm=(1, 2),
        flops=2 * rows * rows * 2 * cases,
    )(nodes, resid_near, resid_far[0])
    if folded:
        sent = call(functools.partial(last_kernel, rank, owned), shape((parts, 1, LANES), F32))(
            part, coef_mine, scale_mine
        )
        coef_out = call(finish_kernel, shape((owned, cases), F32))(exchange(sent))
    else:
        coef_out = lax.dynamic_slice_in_dim(coef, lax.axis_index("dom") * owned, owned, 0)
    return coef_out, nodal_residual


def solution(mesh):
    return jax.shard_map(
        on_device,
        mesh=mesh,
        in_specs=(
            P("dom", None),
            P("dom", None),
            P("dom"),
            P("dom", None),
            P("dom"),
            P("dom", None),
            P("dom"),
            P("dom"),
        ),
        out_specs=(P("dom", None), P("dom", None)),
        check_vma=False,
    )
```

```python
import functools
import math

import jax
import jax.numpy as jnp
from jax import lax
from jax.experimental import pallas as pl
from jax.experimental.pallas import tpu as pltpu
from jax.sharding import PartitionSpec as P

STEP_SIZE = 0.5
SHEAR_MODULUS = 1.0
LAME_FIRST = 1.5
HARDENING = 0.5
YIELD_STRESS = 3.0
EPSILON = 1e-05
ITERS = 2
LANES = 128
SUB = 8
F32 = jnp.float32
BF16 = jnp.bfloat16


def grid_of(node_count, halo_count, elem_count):
    layers = node_count // halo_count
    assert layers == 2
    total = halo_count + 1 - elem_count // layers
    root = math.isqrt(total * total - 4 * halo_count)
    gx = (total + root) // 2
    gy = halo_count // gx
    assert gx * gy == halo_count and (gx - 1) * (gy - 1) * layers == elem_count
    assert gx == gy and gy % SUB == 0
    return gx, gy


def grid_index(p, gx, gy):
    nb = gy // SUB
    q, s = p // SUB, p % SUB
    return (nb * s + q // gx) * gx + q % gx


def column_of(row):
    n = row.shape[1]
    eye = lax.broadcasted_iota(jnp.int32, (n, n), 0) == lax.broadcasted_iota(jnp.int32, (n, n), 1)
    return jnp.sum(jnp.where(eye, row, 0.0), axis=1, keepdims=True)


def row_of(col):
    n = col.shape[0]
    eye = lax.broadcasted_iota(jnp.int32, (n, n), 0) == lax.broadcasted_iota(jnp.int32, (n, n), 1)
    return jnp.sum(jnp.where(eye, col, 0.0), axis=0, keepdims=True)


def split2(value):
    high = value.astype(BF16).astype(F32)
    return high, value - high


def first_layer_column(halo_row, gx, gy):
    n = gx * gy
    want = grid_index(lax.broadcasted_iota(jnp.int32, (n, n), 0), gx, gy)
    hit = lax.broadcasted_iota(jnp.int32, (n, n), 1) == want
    return jnp.sum(jnp.where(hit, halo_row, 0.0), axis=1, keepdims=True)


def select_rows(node_col, i, rows):
    n = node_col.shape[0]
    pick = (3.0 * node_col + i).astype(jnp.int32)
    return jnp.where(lax.broadcasted_iota(jnp.int32, (n, rows), 1) == pick, 1.0, 0.0).astype(BF16)


def scale_block(node_row, i, scale_col, tile, flag_row):
    tiles, n = scale_col.shape[0], node_row.shape[1]
    row = 3.0 * node_row + i
    low = lax.broadcasted_iota(jnp.int32, (tiles, n), 0).astype(F32) * tile
    scale = jnp.sum(jnp.where((row >= low) & (row < low + tile), scale_col, 0.0), axis=0, keepdims=True)
    high, rest = split2(scale)
    middle, last = split2(rest)
    place = lax.broadcasted_iota(jnp.int32, (SUB, n), 0)
    block = jnp.zeros((SUB, n), F32)
    for index, value in enumerate((high, middle, last, flag_row)):
        block = jnp.where(place == index, value, block)
    return block.astype(BF16)


def start_copies(sources, targets, sems):
    copies = [pltpu.make_async_copy(a, b, sems.at[i]) for i, (a, b) in enumerate(zip(sources, targets))]
    for copy in copies:
        copy.start()
    return copies


def spread_kernel(parts, coef_hbm, precond_hbm, out_hbm, high_ref, rest_ref, out_sems, coef_ref, precond_ref, sems):
    owned, cases = coef_ref.shape
    per, spans = cases // parts, LANES // owned
    for copy in start_copies((coef_hbm, precond_hbm), (coef_ref, precond_ref), sems):
        copy.wait()
    high, low = split2(coef_ref[...])
    high_ref[...] = jnp.broadcast_to(high.astype(BF16)[None], (parts, owned, cases))
    (high_copy,) = start_copies((high_ref,), (out_hbm.at[:, :owned, :],), out_sems)
    mine = lax.rem(lax.axis_index("dom"), spans)
    lane = lax.broadcasted_iota(jnp.int32, (1, LANES), 1) // owned
    low = jnp.concatenate([low] * spans, axis=0).T
    low = jnp.where(lane == mine, low, 0.0).astype(BF16)
    rest = jnp.dot(fold_matrix(parts, per, 0), low, preferred_element_type=F32)
    scale = jnp.where(lane == mine, jnp.concatenate([precond_ref[...]] * spans, axis=1), 0.0)
    first, scale = split2(scale)
    second, third = split2(scale)
    row = lax.rem(lax.broadcasted_iota(jnp.int32, (parts * SUB, LANES), 0), SUB) - per
    rest = rest + jnp.where(row == 0, first, jnp.where(row == 1, second, jnp.where(row == 2, third, 0.0)))
    rest_ref[...] = rest.reshape(parts, SUB, LANES).astype(BF16)
    rest_copy = pltpu.make_async_copy(rest_ref, out_hbm.at[:, owned:, :], out_sems.at[1])
    rest_copy.start()
    high_copy.wait()
    rest_copy.wait()


def unfold_matrix(parts, per, half):
    cases = parts * per
    c = lax.broadcasted_iota(jnp.int32, (cases, parts * SUB), 0)
    row = lax.broadcasted_iota(jnp.int32, (cases, parts * SUB), 1)
    return jnp.where(row == (c // per) * SUB + lax.rem(c, per) + half * per, 1.0, 0.0)


def fold_matrix(parts, per, half):
    row = lax.broadcasted_iota(jnp.int32, (parts * SUB, parts * per), 0)
    case = lax.broadcasted_iota(jnp.int32, (parts * SUB, parts * per), 1)
    place = row % SUB - half * per
    here = (place >= 0) & (place < per) & (case == row // SUB * per + place)
    return jnp.where(here, 1.0, 0.0).astype(BF16)


def setup_kernel(
    gx, gy, tile, halo_hbm, scale_hbm, conn_hbm, plastic_hbm, ext_hbm, basis_hbm,
    out_ref, scale_out_ref, ext_out, flag_row_ref, node_ref,
    ext_grid_ref, pick_ref, out_sems, halo_ref, scale_ref, conn_ref, plastic_ref, ext_ref, basis_ref, sems,
):
    n = gx * gy
    rows, rank = basis_ref.shape
    copies = start_copies(
        (halo_hbm, scale_hbm, conn_hbm, plastic_hbm, ext_hbm, basis_hbm),
        (halo_ref, scale_ref, conn_ref, plastic_ref, ext_ref, basis_ref),
        sems,
    )
    for copy in copies[:4]:
        copy.wait()
    conn = conn_ref[...].astype(F32)
    elems = conn.shape[1]
    place = grid_index(lax.broadcasted_iota(jnp.int32, (n, elems), 0), gx, gy).astype(F32) + 2 * n
    node0 = first_layer_column(halo_ref[...].astype(F32), gx, gy)
    node1 = jnp.full((n, 1), -1.0, F32)
    for corner in range(4):
        hit = conn[4 + corner : 5 + corner, :] == place
        found = jnp.max(jnp.where(hit, conn[corner : corner + 1, :], -1.0), axis=1, keepdims=True)
        node1 = jnp.maximum(node1, found)
    active = (plastic_ref[...] == 1).astype(F32)
    cells = (conn[0:1, :] == jnp.broadcast_to(node0, (n, elems)), conn[4:5, :] == place)
    flags = [jnp.max(jnp.where(hit, active, 0.0), axis=1, keepdims=True) for hit in cells]
    flag_row_ref[...] = jnp.zeros_like(flag_row_ref)
    flag_rows = [row_of(flag) for flag in flags]
    flag = flag_rows[1]
    scale_col = column_of(scale_ref[...])
    node_rows = [row_of(node0), row_of(node1)]
    for row in range(n // LANES):
        flag_row_ref[row : row + 1, :] = flag[:, row * LANES : (row + 1) * LANES]
    node_ref[...] = jnp.concatenate(node_rows, axis=1)
    copies[4].wait()
    high, low = split2(ext_ref[...])
    cases = ext_ref.shape[1]
    loads = jnp.concatenate([high.astype(BF16), low.astype(BF16)], axis=1)
    for layer, node in enumerate((node0, node1)):
        for i in range(3):
            start = (3 * layer + i) * n
            pick_ref[start : start + n, :] = select_rows(node, i, rows)
            scale_out_ref[layer, :, i * n : (i + 1) * n] = scale_block(
                node_rows[layer], i, scale_col, tile, flag_rows[layer]
            )
    both = jnp.dot(pick_ref[...], loads, preferred_element_type=F32)
    ext_grid_ref[...] = both[:, :cases] + both[:, cases:]
    out_copies = start_copies((ext_grid_ref,), (ext_out,), out_sems)
    copies[5].wait()
    for part in range(0, rank, 256):
        out_ref[:, part : part + 256] = jnp.dot(
            pick_ref[...], basis_ref[:, part : part + 256], preferred_element_type=F32
        ).astype(BF16)
    for copy in out_copies:
        copy.wait()


def cell_forces(gx, nb, flag_ref, below, above, add_below, add_above):
    quarter = 0.25
    n = gx * nb * SUB

    def load(ref, first, x, yb):
        start = first + (yb * gx + x) * SUB
        return ref[start : start + SUB, :]

    def level(x):
        total, jump = [], []
        for i in range(3):
            low = [load(below[0], below[1] + i * n, x, yb) for yb in range(nb)]
            high = [load(above[0], above[1] + i * n, x, yb) for yb in range(nb)]
            total.append([a + b for a, b in zip(low, high)])
            jump.append([b - a for a, b in zip(low, high)])
        return total, jump

    def roll_up(v):
        return pltpu.roll(v, SUB - 1, 0)

    def roll_down(v):
        return pltpu.roll(v, 1, 0)

    inside = lax.broadcasted_iota(jnp.int32, (SUB, LANES), 0) < SUB - 1
    total_modulus = 2.0 * SHEAR_MODULUS + HARDENING
    here = level(0)
    carry = None
    for x in range(gx - 1):
        there = level(x + 1)
        grad = [[[None] * 3 for _ in range(3)] for _ in range(nb)]
        for i in range(3):
            sum_x = [a + b for a, b in zip(here[0][i], there[0][i])]
            dif_x = [b - a for a, b in zip(here[0][i], there[0][i])]
            jmp_x = [a + b for a, b in zip(here[1][i], there[1][i])]
            sum_n = sum_x[1:] + [roll_up(sum_x[0])]
            dif_n = dif_x[1:] + [roll_up(dif_x[0])]
            jmp_n = jmp_x[1:] + [roll_up(jmp_x[0])]
            for yb in range(nb):
                grad[yb][i][0] = dif_x[yb] + dif_n[yb]
                grad[yb][i][1] = sum_n[yb] - sum_x[yb]
                grad[yb][i][2] = jmp_x[yb] + jmp_n[yb]
        stress = []
        for yb in range(nb):
            g = grad[yb]
            vol = (g[0][0] + g[1][1] + g[2][2]) * quarter
            third = vol * (2.0 * SHEAR_MODULUS / 3.0)
            diag = [g[i][i] * (2.0 * SHEAR_MODULUS * quarter) - third for i in range(3)]
            off = [
                (g[i][j] + g[j][i]) * (SHEAR_MODULUS * quarter) for i, j in ((0, 1), (0, 2), (1, 2))
            ]
            norm = diag[0] * diag[0] + diag[1] * diag[1] + diag[2] * diag[2]
            norm = norm + 2.0 * (off[0] * off[0] + off[1] * off[1] + off[2] * off[2])
            ratio = YIELD_STRESS * lax.rsqrt(jnp.maximum(norm, YIELD_STRESS * YIELD_STRESS))
            soft = HARDENING / total_modulus + (2.0 * SHEAR_MODULUS / total_modulus) * ratio
            factor = jnp.where(load(flag_ref, 0, x, yb) > 0.5, soft, 1.0)
            mean = LAME_FIRST * vol
            s = [None] * 6
            for i in range(3):
                s[i] = (mean + factor * diag[i]) * quarter
                s[3 + i] = factor * off[i] * quarter
            if yb == nb - 1:
                s = [jnp.where(inside, v, 0.0) for v in s]
            stress.append([[s[0], s[3], s[4]], [s[3], s[1], s[5]], [s[4], s[5], s[2]]])
        new_carry = []
        for i in range(3):
            ax = [stress[yb][i][0] for yb in range(nb)]
            ay = [stress[yb][i][1] for yb in range(nb)]
            az = [stress[yb][i][2] for yb in range(nb)]
            ax_p = [roll_down(ax[-1])] + ax[:-1]
            ay_p = [roll_down(ay[-1])] + ay[:-1]
            az_p = [roll_down(az[-1])] + az[:-1]
            for yb in range(nb):
                fx = ax_p[yb] + ax[yb]
                fy = ay_p[yb] - ay[yb]
                fz = az_p[yb] + az[yb]
                back, front = fy - fx, fy + fx
                low, high = back - fz, back + fz
                if carry is not None:
                    low, high = low + carry[i * nb + yb][0], high + carry[i * nb + yb][1]
                if add_below is not None:
                    add_below(i, x, yb, low)
                if add_above is not None:
                    add_above(i, x, yb, high)
                new_carry.append((front - fz, front + fz))
        carry = new_carry
        here = there
    for i in range(3):
        for yb in range(nb):
            if add_below is not None:
                add_below(i, gx - 1, yb, carry[i * nb + yb][0])
            if add_above is not None:
                add_above(i, gx - 1, yb, carry[i * nb + yb][1])


def along_lanes(block, first, count):
    row = lax.broadcasted_iota(jnp.int32, (SUB, LANES), 0)
    mask = jnp.where((row >= first) & (row < first + count), 1.0, 0.0).astype(BF16)
    return lax.dot_general(block, mask, (((0,), (0,)), ((), ())), preferred_element_type=F32)


def scale_of(scale_ref, layer):
    return along_lanes(scale_ref[layer], 0, 3)


def flag_of(scale_ref, layer, n):
    return along_lanes(scale_ref[layer, :, :n], 3, 1)


def times_transposed(a, b):
    return lax.dot_general(a, b, (((1,), (1,)), ((), ())), preferred_element_type=F32)


def rows_of(layer, rows):
    return pl.ds(pl.multiple_of(layer * rows, rows), rows)


def lift_layer(folded, coef, basis_ref, scale_ref, layer, disp_ref, send_ref, flag_row_ref):
    rows = basis_ref.shape[0] // 2
    block = basis_ref[rows_of(layer, rows), :]
    if folded:
        lifted = times_transposed(block, coef)
    else:
        lifted = jnp.dot(block, coef, preferred_element_type=F32)
    disp = lifted * scale_of(scale_ref, layer)
    disp_ref[...] = disp
    send_ref[:rows, :] = disp.astype(BF16)
    send_ref[rows:, :] = flag_row_ref[...].astype(BF16)


def far_kernel(same_ref, other_ref, basis_ref, scale_ref, flag_row_ref, disp_ref, send_ref, coef_ref, source_ref):
    rank = basis_ref.shape[1]
    chips, _, half = same_ref.shape
    core = lax.rem(lax.axis_index("dom"), 2)
    source_ref[:, core] = same_ref[...]
    source_ref[:, 1 - core] = other_ref[...]
    coef = source_ref[...].reshape(chips * 2 * SUB, half)
    per = SUB * half // rank
    for part in range(2):
        turn = unfold_matrix(2 * chips, per, part).astype(BF16)
        coef_ref[:, part * half : (part + 1) * half] = jnp.dot(
            turn, coef, preferred_element_type=F32
        ).astype(BF16)
    lift_layer(True, coef_ref[...], basis_ref, scale_ref, core, disp_ref, send_ref, flag_row_ref)


def first_far_kernel(owned, source_ref, basis_ref, scale_ref, flag_row_ref, disp_ref, send_ref, coef_ref):
    coef_ref[...] = source_ref[:, :owned, :].reshape(coef_ref.shape)
    odd = lax.rem(lax.axis_index("dom"), 2)
    lift_layer(False, coef_ref[...], basis_ref, scale_ref, odd, disp_ref, send_ref, flag_row_ref)


def near_kernel(folded, coef_ref, basis_ref, scale_ref, flag_row_ref, disp_ref, send_ref):
    odd = lax.rem(lax.axis_index("dom"), 2)
    lift_layer(folded, coef_ref[...], basis_ref, scale_ref, 1 - odd, disp_ref, send_ref, flag_row_ref)


def putter(gx, n, f_ref, layer):
    def put(i, x, yb, value):
        start = (3 * layer + i) * n + (yb * gx + x) * SUB
        f_ref[start : start + SUB, :] = value

    return put


def own_kernel(gx, gy, rank, prepare, far_ref, near_ref, scale_in_ref, *refs):
    if prepare:
        start_ref, disp_ref, force_ref, coef_ref, scale_ref, flag_ref = refs
    else:
        disp_ref, force_ref, flag_ref = refs
    n, nb = gx * gy, gy // SUB
    flag_ref[...] = flag_of(scale_in_ref, 0, n)
    even = lax.rem(lax.axis_index("dom"), 2) == 0
    far, near = far_ref[...], near_ref[...]
    disp_ref[: 3 * n, :] = jnp.where(even, far, near)
    disp_ref[3 * n :, :] = jnp.where(even, near, far)
    put = functools.partial(putter, gx, n, force_ref)
    cell_forces(gx, nb, flag_ref, (disp_ref, 0), (disp_ref, 3 * n), put(0), put(1))
    if prepare:
        parts, depth, cases = start_ref.shape
        owned, per, spans = depth - SUB, cases // parts, LANES * parts // rank
        me = lax.axis_index("dom")
        rest = start_ref[:, owned:, :].astype(F32)
        rest = [jnp.sum(rest[k * spans : (k + 1) * spans], axis=0) for k in range(parts // spans)]
        rest = jnp.concatenate(rest, axis=1)
        pick = lax.broadcasted_iota(jnp.int32, (SUB, cases), 0)
        lane = lax.broadcasted_iota(jnp.int32, (SUB, cases), 1)
        pick = jnp.where((lane == pick + me * per) & (pick < per), 1.0, 0.0).astype(BF16)
        high = times_transposed(pick, start_ref[:, :owned, :].reshape(rank, cases))
        scale = jnp.sum(rest[per : per + 3, :], axis=0, keepdims=True)
        scale_ref[...] = fold(jnp.broadcast_to(scale, (SUB, rank)))
        coef_ref[...] = fold(high + rest)


def side_cells(gx, gy, remote_ref, is_next, disp_ref, flag, side_ref, side_flag_ref, force_ref):
    n, nb = gx * gy, gy // SUB
    layer = 3 * n
    remote = remote_ref[...].astype(F32)
    side_ref[:layer, :] = jnp.where(is_next, disp_ref[layer:, :], remote[:layer, :])
    side_ref[layer:, :] = jnp.where(is_next, remote[:layer, :], disp_ref[:layer, :])
    for row in range(n // LANES):
        theirs = column_of(remote[layer + row : layer + row + 1, :])
        where = slice(row * LANES, (row + 1) * LANES)
        side_flag_ref[where, :] = jnp.where(is_next, flag[where, :], jnp.broadcast_to(theirs, (LANES, LANES)))
    chosen = jnp.broadcast_to(is_next, (SUB, LANES))
    put = putter(gx, n, force_ref, 0)
    lows = {}

    def keep(i, x, yb, value):
        lows[i, x, yb] = value

    def choose(i, x, yb, value):
        put(i, x, yb, jnp.where(chosen, lows.pop((i, x, yb)), value))

    cell_forces(gx, nb, side_flag_ref, (side_ref, 0), (side_ref, layer), keep, choose)


def project(resid, basis_ref, scale_ref, layer, parts, scaled_ref):
    rows = resid.shape[0]
    rank = basis_ref.shape[1]
    block = basis_ref[rows_of(layer, rows), :]
    scaled_ref[...] = (resid * scale_of(scale_ref, layer)).astype(BF16)
    if parts is None:
        return jnp.dot(scaled_ref[...].astype(F32).T.astype(BF16), block, preferred_element_type=F32)
    half, per = rank // 2, resid.shape[1] // parts
    total = None
    for part in range(2):
        turn = fold_matrix(parts, per, part)
        turned = times_transposed(turn, scaled_ref[...]).astype(BF16)
        term = jnp.dot(turned, block[:, part * half : (part + 1) * half], preferred_element_type=F32)
        total = term if total is None else total + term
    return total


def side_kernel(
    gx, gy, parts, remote_ref, disp_ref, force_ref, basis_ref, scale_ref, ext_hbm,
    resid_hbm, rest_ref, total_ref, side_ref, side_flag_ref, near_force_ref, scaled_ref, resid_ref, out_sems, ext_ref, sems,
):
    layer = 3 * gx * gy
    copies = start_copies((ext_hbm,), (ext_ref,), sems)
    odd = lax.rem(lax.axis_index("dom"), 2)
    flag = flag_of(scale_ref, 1, gx * gy)
    side_cells(gx, gy, remote_ref, odd == 0, disp_ref, flag, side_ref, side_flag_ref, near_force_ref)
    copies[0].wait()
    near_rows, far_rows = rows_of(1 - odd, layer), rows_of(odd, layer)
    rest_ref[...] = ext_ref[far_rows, :] - force_ref[far_rows, :]
    resid_ref[...] = ext_ref[near_rows, :] - force_ref[near_rows, :] - near_force_ref[...]
    out_copies = start_copies((resid_ref,), (resid_hbm,), out_sems)
    total_ref[...] = project(resid_ref[...], basis_ref, scale_ref, 1 - odd, parts, scaled_ref)
    out_copies[0].wait()


def sweep_kernel(gx, gy, parts, remote_ref, disp_ref, rest_ref, total_ref, basis_ref, scale_ref, *refs):
    part_ref, *resid_hbm, side_ref, side_flag_ref, far_force_ref, scaled_ref, resid_ref, out_sems = refs
    me = lax.axis_index("dom")
    odd = lax.rem(me, 2)
    flag = flag_of(scale_ref, 1, gx * gy)
    side_cells(gx, gy, remote_ref, odd == 1, disp_ref, flag, side_ref, side_flag_ref, far_force_ref)
    resid = rest_ref[...] - jnp.where(me > 0, far_force_ref[...], 0.0)
    resid_ref[...] = resid
    out_copies = start_copies([resid_ref] * len(resid_hbm), resid_hbm, out_sems)
    total = total_ref[...] + project(resid, basis_ref, scale_ref, odd, parts, scaled_ref)
    part_ref[...] = total.reshape(part_ref.shape).astype(part_ref.dtype)
    for copy in out_copies:
        copy.wait()


def fold(value):
    half = value.shape[1] // 2
    row = lax.broadcasted_iota(jnp.int32, (SUB, half), 0)
    return jnp.where(row < SUB // 2, value[:, :half], pltpu.roll(value[:, half:], SUB // 2, 0))


def step(coef, update, rank):
    square = jnp.broadcast_to(jnp.sum(update * update, axis=1, keepdims=True), (SUB, LANES))
    square = (square + pltpu.roll(square, SUB // 2, 0))[:, 0:1]
    return coef + STEP_SIZE * update * lax.rsqrt(square / rank + EPSILON)


def middle_kernel(rank, parts_ref, start_ref, scale_ref, coef_ref, send_ref):
    update = scale_ref[...] * jnp.sum(parts_ref[...].astype(F32), axis=0)
    coef = step(start_ref[...], update, rank)
    coef_ref[...] = coef
    send_ref[...] = jnp.broadcast_to(coef.astype(BF16)[None], send_ref.shape)


def last_kernel(rank, owned, parts_ref, coef_ref, scale_ref, send_ref):
    update = scale_ref[...] * jnp.sum(parts_ref[...].astype(F32), axis=0)
    coef = step(coef_ref[...], update, rank)
    parts, spans = send_ref.shape[0], LANES // owned
    half = SUB // 2
    place = lax.broadcasted_iota(jnp.int32, (SUB, LANES), 1) // owned
    column = lax.rem(lax.broadcasted_iota(jnp.int32, (SUB, LANES), 0), half)
    for block in range(coef.shape[1] // LANES):
        value = coef[:, block * LANES : (block + 1) * LANES]
        turned = [value] + [pltpu.roll(value, shift * owned, 1) for shift in range(1, spans)]
        for span in range(spans):
            line = jnp.zeros_like(value)
            for shift in range(spans):
                line = jnp.where(lax.rem(column + spans - span, spans) == shift, turned[shift], line)
            line = jnp.where(place == column, line, 0.0)
            device = block * spans + span
            send_ref[device] = jnp.sum(line[:half], axis=0, keepdims=True)
            send_ref[parts // 2 + device] = jnp.sum(line[half:], axis=0, keepdims=True)


def finish_kernel(got_ref, out_ref):
    owned, cases = out_ref.shape
    parts = got_ref.shape[0]
    per = cases // parts
    got = jnp.concatenate([got_ref[source] for source in range(parts)], axis=0)
    got = jnp.concatenate([got] * per, axis=0).T
    place = lax.broadcasted_iota(jnp.int32, (owned, LANES), 1) // parts
    line = jnp.zeros((owned, LANES), F32)
    for column in range(per):
        line = jnp.where(place == column, got[column * owned : (column + 1) * owned, :], line)
    place = lax.broadcasted_iota(jnp.int32, (LANES, cases), 0)
    case = lax.broadcasted_iota(jnp.int32, (LANES, cases), 1)
    turn = jnp.where(case == lax.rem(place, parts) * per + place // parts, 1.0, 0.0).astype(BF16)
    high, rest = split2(line)
    middle, low = split2(rest)
    value = jnp.concatenate([high.astype(BF16), middle.astype(BF16), low.astype(BF16)], axis=0)
    turned = jnp.dot(value, turn, preferred_element_type=F32)
    out_ref[...] = turned[:owned] + turned[owned : 2 * owned] + turned[2 * owned :]


def unpermute_kernel(gx, gy, node_ref, near_hbm, far_hbm, out_ref, parts_ref, near_ref, far_ref, sems):
    n = gx * gy
    rows, cases = out_ref.shape
    copies = start_copies((near_hbm, far_hbm), (near_ref, far_ref), sems)
    node = node_ref[...]
    target = jnp.concatenate(
        [3.0 * node[:, layer * n : (layer + 1) * n] + i for layer in range(2) for i in range(3)], axis=1
    ).astype(jnp.int32)
    step = rows // 3
    picks = [
        jnp.where(lax.broadcasted_iota(jnp.int32, (step, rows), 0) + start == target, 1.0, 0.0).astype(BF16)
        for start in range(0, rows, step)
    ]
    odd = lax.rem(lax.axis_index("dom"), 2)
    for copy, ref, layer in zip(copies, (near_ref, far_ref), (1 - odd, odd)):
        copy.wait()
        high, low = split2(ref[...])
        parts_ref[rows_of(layer, 3 * n), :cases] = high.astype(BF16)
        parts_ref[rows_of(layer, 3 * n), cases:] = low.astype(BF16)
    for i, pick in enumerate(picks):
        both = jnp.dot(pick, parts_ref[...], preferred_element_type=F32)
        out_ref[i * step : (i + 1) * step, :] = both[:, :cases] + both[:, cases:]


def call(kernel, outs, scratch=(), hbm=(), hbm_out=(), vmem=24, flops=0, nbytes=0):
    def run(*operands):
        shapes = [operands[i].shape for i in hbm]
        operands = [
            pltpu.with_memory_space_constraint(value, pltpu.HBM) if i in hbm else value
            for i, value in enumerate(operands)
        ]
        spaces = [pltpu.HBM if i in hbm else pltpu.VMEM for i in range(len(operands))]
        places = [
            pl.BlockSpec(memory_space=pltpu.HBM if i in hbm_out else pltpu.VMEM)
            for i in range(len(outs) if isinstance(outs, tuple) else 1)
        ]
        return pl.pallas_call(
            kernel,
            out_shape=outs,
            in_specs=[pl.BlockSpec(memory_space=space) for space in spaces],
            out_specs=tuple(places) if isinstance(outs, tuple) else places[0],
            scratch_shapes=[
                *scratch,
                *[pltpu.VMEM(shape, operands[i].dtype) for i, shape in zip(hbm, shapes)],
                *([pltpu.SemaphoreType.DMA((len(hbm),))] if hbm else []),
            ],
            compiler_params=pltpu.CompilerParams(vmem_limit_bytes=vmem << 20),
            cost_estimate=pl.CostEstimate(flops=flops, bytes_accessed=nbytes, transcendentals=0),
        )(*operands)

    return run


def on_device(coef_init, basis, basis_scale, ext_force, precond, connectivity, halo_nodes, plastic):
    parts = lax.axis_size("dom")
    rows, cases = ext_force.shape
    rank = basis.shape[1]
    owned = coef_init.shape[0]
    n = halo_nodes.shape[0]
    elems = connectivity.shape[0]
    gx, gy = grid_of(rows // 3, n, elems)
    tile = rows // basis_scale.shape[0]
    half = rank // 2
    layer = 3 * n
    folded = parts * (SUB // 2) == cases and LANES % owned == 0 and owned * (SUB // 2) == LANES
    shape = jax.ShapeDtypeStruct
    scratch = pltpu.VMEM

    chips = parts // 2
    near_pairs = [(d, d ^ 1) for d in range(parts)]

    def exchange(value):
        return lax.all_to_all(value, "dom", 0, 0)

    def exchange_chips(value):
        groups = [list(range(core, parts, 2)) for core in range(2)]
        return lax.all_to_all(value, "dom", 0, 0, axis_index_groups=groups)

    if folded:
        start = exchange(
            call(
                functools.partial(spread_kernel, parts),
                pltpu.HBM((parts, owned + SUB, cases), BF16),
                [
                    scratch((parts, owned, cases), BF16),
                    scratch((parts, SUB, cases), BF16),
                    pltpu.SemaphoreType.DMA((2,)),
                ],
                hbm=(0, 1),
                hbm_out=(0,),
            )(coef_init, precond.reshape(1, owned))
        )
    else:
        coef = lax.all_gather(coef_init, "dom", axis=0, tiled=True)
        scaling = lax.all_gather(precond, "dom", axis=0, tiled=True)
    basis_grid, scale_grid, ext_grid, flag_row, nodes = call(
        functools.partial(setup_kernel, gx, gy, tile),
        (
            shape((rows, rank), BF16),
            shape((2, SUB, layer), BF16),
            pltpu.HBM((rows, cases), F32),
            shape((SUB, LANES), F32),
            shape((1, 2 * n), F32),
        ),
        [scratch((rows, cases), F32), scratch((rows, rows), BF16), pltpu.SemaphoreType.DMA((1,))],
        hbm=(0, 1, 2, 3, 4, 5),
        hbm_out=(2,),
        flops=2 * rows * rows * (rank + 2 * cases),
        nbytes=4 * rows * rank,
    )(
        halo_nodes.reshape(1, n),
        basis_scale.reshape(1, -1),
        connectivity.T,
        plastic.reshape(1, elems),
        ext_force,
        basis,
    )
    far_pairs = [pair for d in range(1, parts - 1, 2) for pair in ((d, d + 1), (d + 1, d))]
    layer_disp, layer_sent = shape((layer, cases), F32), shape((layer + SUB, cases), BF16)
    side_scratch = [scratch((2 * layer, cases), F32), scratch((n, LANES), F32)]
    columns = shape((SUB, half), F32)
    for sweep in range(ITERS):
        second, last = folded and sweep > 0, sweep == ITERS - 1
        first_source = start if folded else coef.astype(BF16).reshape(parts, owned, cases)
        source = send if second else (first_source,)
        far_disp, far, coef_rows = call(
            far_kernel if second else functools.partial(first_far_kernel, owned),
            (layer_disp, layer_sent, shape((cases, rank) if second else (rank, cases), BF16)),
            [scratch((chips, 2, SUB, half), BF16)] if second else (),
            flops=rows * rank * cases,
        )(*source, basis_grid, scale_grid, flag_row)
        far = lax.ppermute(far, "dom", far_pairs)
        near_disp, near = call(
            functools.partial(near_kernel, second), (layer_disp, layer_sent), flops=rows * rank * cases
        )(coef_rows, basis_grid, scale_grid, flag_row)
        near = lax.ppermute(near, "dom", near_pairs)
        prepare = folded and sweep == 0
        disp, force, *mine = call(
            functools.partial(own_kernel, gx, gy, rank, prepare),
            (shape((rows, cases), F32), shape((rows, cases), F32), *([columns] * 2 if prepare else [])),
            [scratch((n, LANES), F32)],
            flops=rows * rank * cases,
        )(far_disp, near_disp, scale_grid, *([start] if prepare else []))
        if prepare:
            coef_mine, scale_mine = mine
        cut = parts if folded else None
        total_shape = (parts * SUB, half) if folded else (cases, rank)
        layer_scratch = [
            *side_scratch,
            scratch((layer, cases), F32),
            scratch((layer, cases), BF16),
            scratch((layer, cases), F32),
            pltpu.SemaphoreType.DMA((1,)),
        ]
        resid_near, rest, total = call(
            functools.partial(side_kernel, gx, gy, cut),
            (pltpu.HBM((layer, cases), F32), layer_disp, shape(total_shape, F32)),
            layer_scratch,
            hbm=(5,),
            hbm_out=(0,),
            flops=rows * rank * cases,
        )(near, disp, force, basis_grid, scale_grid, ext_grid)
        part_shape = shape((parts, SUB, half), BF16) if folded else shape((cases, rank), F32)
        part, *resid_far = call(
            functools.partial(sweep_kernel, gx, gy, cut),
            (part_shape, *([pltpu.HBM((layer, cases), F32)] if last else [])),
            layer_scratch,
            hbm_out=(1,) if last else (),
            flops=2 * rows * rank * cases,
        )(far, disp, rest, total, basis_grid, scale_grid)
        if folded:
            part = exchange(part)
            if not last:
                coef_mine, send = call(
                    functools.partial(middle_kernel, rank), (columns, shape((chips, SUB, half), BF16))
                )(part, coef_mine, scale_mine)
                send = exchange_chips(send)
                send = send, lax.ppermute(send, "dom", near_pairs)
        else:
            update = scaling[:, None] * lax.psum(part, "dom").T
            root = jnp.sqrt(jnp.sum(update * update, axis=0) / rank + EPSILON)
            coef = coef + STEP_SIZE * update / root
    nodal_residual = call(
        functools.partial(unpermute_kernel, gx, gy),
        shape((rows, cases), F32),
        [scratch((rows, 2 * cases), BF16)],
        hbm=(1, 2),
        flops=2 * rows * rows * 2 * cases,
    )(nodes, resid_near, resid_far[0])
    if folded:
        sent = call(functools.partial(last_kernel, rank, owned), shape((parts, 1, LANES), F32))(
            part, coef_mine, scale_mine
        )
        coef_out = call(finish_kernel, shape((owned, cases), F32))(exchange(sent))
    else:
        coef_out = lax.dynamic_slice_in_dim(coef, lax.axis_index("dom") * owned, owned, 0)
    return coef_out, nodal_residual


def solution(mesh):
    return jax.shard_map(
        on_device,
        mesh=mesh,
        in_specs=(
            P("dom", None),
            P("dom", None),
            P("dom"),
            P("dom", None),
            P("dom"),
            P("dom", None),
            P("dom"),
            P("dom"),
        ),
        out_specs=(P("dom", None), P("dom", None)),
        check_vma=False,
    )
```
